32 devices in a mesh: gz: 8 (over z, x), gy: 4 (over y, core).
Axes of the slice: x: 2, y: 2, z: 4, core: 2. Of those that a mesh axis runs over, the one named last changes fastest.
Arguments:
- spectrum: float32 [3, 2, 4, 512, 4096], P(None, None, None, 'gy', 'gz'), may hold values from -6 to 6
- cells: int32 [2, 65536], P(None, ('gz', 'gy')), may hold values from 0 to 4095, as said below
- offsets: float32 [3, 65536], P(None, ('gz', 'gy')), may hold values from 0 to 1
- counts: int32 [32], P(('gz', 'gy')), may hold values from 1 to 2048, as said below
Outputs:
- coefficients: float32 [3, 4, 512, 4096], P(None, None, 'gy', 'gz')
- interpolated: float32 [3, 65536], P(None, ('gz', 'gy'))
The draws below stay inside these ranges and needn't reach their ends.
Inputs may be any that keep to these rules, and one draw needn't show every extreme that they name: The particles of device number b = i * (size of gy) + j, at gz index i and gy index j, occupy slots b * 2048 to b * 2048 + 2047. Their base cells lie from two cells before that device's block to the cell just after its last one: along y from j * 128 - 2 to j * 128 + 128 modulo 512, along z from i * 512 - 2 to i * 512 + 512 modulo 4096. Empty slots hold such cells too. `counts`: live particles of each device fill its first slots; some device has exactly 2048.
All inputs are finite; a program needn't handle non-finite values.
Results may differ from the reference program's by a relative error of at most 0.000096.
Values sent between devices are 32-bit elements; how exact they have to be, the bound alone decides.
A program may use at most 128 MiB of HBM per device.

```python
import math
import jax
import jax.numpy as jnp

NZ = 4096
COMPS = 3
NX = 4
CY = 128
PCAP = 2048
NY = 512
CZ = 512
NDEV = 32
SLOTS = 65536
N_GY = 4


def draw_cells(key, part):
    slot = jnp.arange(SLOTS, dtype=jnp.int32)
    owner = slot // PCAP
    owner_z = owner // N_GY
    owner_y = owner % N_GY
    key_y, key_z = jax.random.split(key)
    shift_y = jax.random.randint(key_y, (SLOTS,), -2, CY + 1, dtype=jnp.int32)
    shift_z = jax.random.randint(key_z, (SLOTS,), -2, CZ + 1, dtype=jnp.int32)
    cell_y = (owner_y * CY + shift_y) % NY
    cell_z = (owner_z * CZ + shift_z) % NZ
    return jnp.stack([cell_y, cell_z]).astype(jnp.int32)


def draw_counts(key, part):
    key_div, key_jit, key_top = jax.random.split(key, 3)
    divisor = jax.random.randint(key_div, (NDEV,), 1, 5, dtype=jnp.int32)
    jitter = jax.random.randint(key_jit, (NDEV,), 0, max(PCAP // 16, 1), dtype=jnp.int32)
    basic = jnp.maximum(PCAP // divisor - jitter, 1)
    fullest = jax.random.randint(key_top, (), 0, NDEV, dtype=jnp.int32)
    return jnp.where(jnp.arange(NDEV, dtype=jnp.int32) == fullest, PCAP, basic).astype(jnp.int32)


def block_levels(stream_key, dims, pieces, low, top_value):
    loudness = 1.0
    for dim, parts in pieces:
        steps = jax.random.uniform(jax.random.fold_in(jax.random.fold_in(stream_key, 6), dim), (parts,), jnp.float32, low / len(pieces), top_value / len(pieces))
        loudness = loudness * jnp.repeat(jnp.exp(steps), dims[dim] // parts).reshape((-1,) + (1,) * (len(dims) - 1 - dim))
    return loudness


def noise(own_key, dims, scale, reach, cuts=(), held_as=jnp.bfloat16):
    factor_of = block_levels(own_key, dims, cuts, -0.22, 0.18) if cuts else 1.0
    drawn = jax.random.normal(own_key, dims, jnp.float32) * scale * factor_of
    return jnp.minimum(jnp.maximum(drawn, -reach), reach).astype(held_as)


def setup_inputs(seed: int = 0) -> dict:
    splits = jax.random.split(jax.random.key(seed), 5)
    return {
        "spectrum": noise(splits[0], (COMPS, 2, NX, NY, NZ), 1.0, 6.0, ((3, 4), (4, 8)), jnp.float32),
        "cells": draw_cells(jax.random.fold_in(splits[4], 71), 0),
        "offsets": jnp.clip(1.0 * jax.random.uniform(splits[2], (3, SLOTS), jnp.float32) ** block_levels(splits[2], (3, SLOTS), ((1, 32),), -0.2, 0.2), 0.0, 1.0),
        "counts": draw_counts(jax.random.fold_in(splits[4], 71), 0),
    }


def spline_weights(frac):
    cube = frac * frac * frac
    square = frac * frac
    first = (1.0 - frac) * (1.0 - frac) * (1.0 - frac) / 6.0
    second = (3.0 * cube - 6.0 * square + 4.0) / 6.0
    third = (-3.0 * cube + 3.0 * square + 3.0 * frac + 1.0) / 6.0
    fourth = cube / 6.0
    return [first, second, third, fourth]

def reference(spectrum, cells, offsets, counts):
    wave = jnp.arange(NZ).astype(spectrum.dtype)
    symbol = (4.0 + 2.0 * jnp.cos(wave * (2.0 * math.pi / NZ))) / 6.0
    factor = 1.0 / (symbol * math.sqrt(NZ))
    real_part = spectrum[:, 0] * factor
    imag_part = spectrum[:, 1] * factor
    complex_hat = real_part + 1j * imag_part
    coefficients = jnp.real(jnp.fft.ifft(complex_hat, axis=-1)) * NZ
    coefficients = coefficients.astype(spectrum.dtype)
    weight_x = spline_weights(offsets[0])
    weight_y = spline_weights(offsets[1])
    weight_z = spline_weights(offsets[2])
    total_sum = jnp.zeros((COMPS, NX, SLOTS), spectrum.dtype)
    for step_y in range(4):
        index_y = ((cells[0] - 1 + step_y) % NY).astype(jnp.int32)
        for step_z in range(4):
            index_z = ((cells[1] - 1 + step_z) % NZ).astype(jnp.int32)
            picked = coefficients[:, :, index_y, index_z]
            total_sum = total_sum + picked * (weight_y[step_y] * weight_z[step_z])[None, None, :]
    values = total_sum[:, 0] * weight_x[0]
    for plane in range(1, 4):
        values = values + total_sum[:, plane] * weight_x[plane]
    slot = jnp.arange(SLOTS, dtype=jnp.int32)
    live_mask = slot % PCAP < counts[slot // PCAP]
    interpolated = jnp.where(live_mask[None, :], values, jnp.zeros_like(values))
    return (coefficients, interpolated)
```

```python
import functools
import math

import jax
import jax.numpy as jnp
import numpy as np
from jax import lax
from jax.experimental import pallas as pl
from jax.experimental.pallas import tpu as pltpu
from jax.sharding import PartitionSpec as P

F32 = jnp.float32
BF16 = jnp.bfloat16


def split(value):
    high = value.astype(BF16)
    return high, (value - high.astype(F32)).astype(BF16)


def split_table(table):
    high = np.asarray(table, np.float32).astype(BF16)
    low = (table - high.astype(np.float64)).astype(np.float32).astype(BF16)
    return high, low


def dot(left, right):
    return jnp.dot(left, right, preferred_element_type=F32)


def dft(items):
    count = len(items)
    if count == 1:
        return items
    even = dft(items[0::2])
    odd = dft(items[1::2])
    half = count // 2
    low, high = [], []
    for m in range(half):
        er, ei = even[m]
        xr, xi = odd[m]
        if m == 0:
            tr, ti = xr, xi
        elif 4 * m == count:
            tr, ti = -xi, xr
        elif 8 * m == count:
            s = math.sqrt(0.5)
            tr, ti = (xr - xi) * s, (xr + xi) * s
        elif 8 * m == 3 * count:
            s = math.sqrt(0.5)
            tr, ti = (xr + xi) * -s, (xr - xi) * s
        else:
            c, s = math.cos(2 * math.pi * m / count), math.sin(2 * math.pi * m / count)
            tr, ti = xr * c - xi * s, xr * s + xi * c
        low.append((er + tr, ei + ti))
        high.append((er - tr, ei - ti))
    return low + high


def line_kernel(re_ref, im_ref, factor_ref, tcos_ref, tsin_ref, whi_ref, wlo_ref, perm_ref,
                out_ref, yhi_ref, ylo_ref, z_ref):
    parts, lines, width = re_ref.shape
    step = 16

    @pl.loop(0, lines // step)
    def _(group):
        rows = pl.ds(pl.multiple_of(group * step, step), step)
        for tile in range(width // 128):
            lanes = slice(tile * 128, tile * 128 + 128)
            items = []
            for i in range(parts):
                f = factor_ref[i : i + 1, lanes]
                items.append((re_ref[i, rows, lanes] * f, im_ref[i, rows, lanes] * f))
            for m, (yr, yi) in enumerate(dft(items)):
                c, s = tcos_ref[m : m + 1, lanes], tsin_ref[m : m + 1, lanes]
                zr, zi = yr * c - yi * s, yr * s + yi * c
                shifted = slice(width + tile * 128, width + tile * 128 + 128)
                hi, lo = split(zr)
                yhi_ref[m, rows, lanes] = hi
                ylo_ref[m, rows, lanes] = lo
                hi, lo = split(zi)
                yhi_ref[m, rows, shifted] = hi
                ylo_ref[m, rows, shifted] = lo

    @pl.loop(0, parts)
    def _(m):
        yhi = yhi_ref[m]
        z_ref[m] = dot(yhi, whi_ref[...]) + dot(ylo_ref[m], whi_ref[...]) + dot(yhi, wlo_ref[...])

    each = width // parts
    for target in range(parts):
        lanes = slice(target * each, target * each + each)
        joined = jnp.concatenate([z_ref[m, :, lanes] for m in range(parts)], axis=1)
        hi, lo = split(joined)
        out_ref[target] = dot(hi, perm_ref[...]) + dot(lo, perm_ref[...])


def transform(real, imag, tables):
    parts, lines, width = real.shape
    return pl.pallas_call(
        line_kernel,
        out_shape=jax.ShapeDtypeStruct((parts, lines, width), F32),
        in_specs=[pl.BlockSpec(memory_space=pltpu.VMEM)] * 8,
        out_specs=pl.BlockSpec(memory_space=pltpu.VMEM),
        scratch_shapes=[
            pltpu.VMEM((parts, lines, 2 * width), BF16),
            pltpu.VMEM((parts, lines, 2 * width), BF16),
            pltpu.VMEM((parts, lines, width), F32),
        ],
        compiler_params=pltpu.CompilerParams(vmem_limit_bytes=24 << 20),
        cost_estimate=pl.CostEstimate(
            flops=20 * parts * lines * width * width, bytes_accessed=12 * parts * lines * width,
            transcendentals=0),
    )(real, imag, *tables)


def line_tables(parts, width):
    length = parts * width
    k = np.arange(length, dtype=np.float64)
    symbol = (4.0 + 2.0 * np.cos(k * (2.0 * math.pi / length))) / 6.0
    factor = (1.0 / (symbol * math.sqrt(length))).reshape(parts, width).astype(np.float32)
    turn = np.outer(np.arange(parts), np.arange(width)) * (2.0 * math.pi / length)
    angle = (np.outer(np.arange(width), np.arange(width)) % width) * (2.0 * math.pi / width)
    whi, wlo = split_table(np.concatenate([np.cos(angle), -np.sin(angle)], axis=0))
    each = width // parts
    perm = np.zeros((width, width), np.float32)
    for m in range(parts):
        for q in range(each):
            perm[m * each + q, parts * q + m] = 1.0
    made = (factor, np.cos(turn).astype(np.float32), np.sin(turn).astype(np.float32),
            whi, wlo, perm.astype(BF16))
    return made


MESH = pl.DeviceIdType.MESH


SUB = 4
DIRECT = 6
AHEAD = 6
LAG = 2
FIRST_RELAYS = 16
RELAYS = 6


def hub_kernel(spec, count_ref, cells, offs, factor, tcos, tsin, whi, wlo, perm, out, vals,
               xbuf, yhi, ylo, zown, zsend, zrecv, total, field, edge_z, halo_z, halo_y, corner,
               fboth, pzhi, pzlo, py, wxs,
               send_a, recv_a, cross_s, cross_r, dist_s, dist_r, loc, keep,
               ez_s, ez_r, ey_s, ey_r, ec_s, ec_r, out_s):
    components, _, planes, rows_y, width = spec.shape
    lines = rows_y // (2 * SUB)
    pieces = components * planes
    chunks = pieces * SUB
    slots = cells.shape[1]
    chunk = 256
    groups = slots // chunk
    share = groups // SUB
    parts = 8
    each = width // parts
    wide = width // 2
    body = rows_y + 16
    me = lax.axis_index("gz")
    half = me // 4
    side = me % 2
    is_hub = ((me // 2) == 1) | ((me // 2) == 2)
    hub_same = 2 + 2 * half + side
    hub_other = 2 + 2 * half + (1 - side)
    leaf_same = 6 * half + side
    leaf_other = 6 * half + (1 - side)
    partner = 4 - 2 * half + side
    z_next, z_prev = lax.rem(me + 1, 8), lax.rem(me + 7, 8)
    gy, gy_count = lax.axis_index("gy"), lax.axis_size("gy")
    y_next, y_prev = lax.rem(gy + 1, gy_count), lax.rem(gy + gy_count - 1, gy_count)
    diagonals = [{"gz": z, "gy": y} for z in (z_next, z_prev) for y in (y_next, y_prev)]

    barrier = pltpu.get_barrier_semaphore()

    def greet(peer):
        pl.semaphore_signal(barrier, inc=1, device_id=peer, device_id_type=MESH)

    for peer in [{"gz": z_next}, {"gz": z_prev}, {"gy": y_next}, {"gy": y_prev}] + diagonals:
        greet(peer)

    @pl.when(is_hub)
    def _():
        for peer in (leaf_same, leaf_other, hub_other, partner):
            greet({"gz": peer})

    @pl.when(jnp.logical_not(is_hub))
    def _():
        for peer in (hub_same, hub_other, leaf_other):
            greet({"gz": peer})

    def rows_of(j, which):
        return pl.ds(pl.multiple_of(which * (lines * SUB) + (j % SUB) * lines, lines), lines)

    def remote(source, target, send, recv, peer):
        return pltpu.make_async_remote_copy(
            src_ref=source, dst_ref=target, send_sem=send, recv_sem=recv,
            device_id=peer if isinstance(peer, dict) else {"gz": peer}, device_id_type=MESH)

    def source(j, which):
        piece = j // SUB
        return spec.at[piece // planes, :, piece % planes, rows_of(j, which), :]

    def give(j, which, n, peer):
        return remote(source(j, which),
                      xbuf.at[j, me % 4], send_a.at[j, n], recv_a.at[j, me % 4], peer)

    def relay(j):
        slot = leaf_other % 4
        return remote(xbuf.at[j, slot], xbuf.at[j, slot], send_a.at[j, 2], recv_a.at[j, slot],
                      hub_same)

    def arrival(j, slot):
        return remote(xbuf.at[j, slot], xbuf.at[j, slot], send_a.at[j, 0], recv_a.at[j, slot],
                      partner)

    def own(j):
        return pltpu.make_async_copy(source(j, side),
                                     xbuf.at[j, me % 4], loc.at[j])

    def cross(j):
        return remote(zsend.at[j], zrecv.at[j], cross_s.at[j], cross_r.at[j], partner)

    def place(j, which):
        return field.at[j // SUB, rows_of(j, which), :]

    def hand(j, n, peer):
        return remote(total.at[j, peer % 4], place(j, side), dist_s.at[j, n],
                      dist_r.at[j, side], peer)

    def taken(j, which):
        return remote(total.at[j, 0], place(j, which), dist_s.at[j, 0], dist_r.at[j, which],
                      hub_other)

    def kept(j):
        return pltpu.make_async_copy(total.at[j, me % 4], place(j, side), keep.at[j])

    def edge_copies(p):
        copies = [
            remote(edge_z.at[p, 0], halo_z.at[p, 0], ez_s.at[p, 0], ez_r.at[p, 0], z_next),
            remote(edge_z.at[p, 1], halo_z.at[p, 1], ez_s.at[p, 1], ez_r.at[p, 1], z_prev),
            remote(field.at[p, rows_y - 8 :, :], halo_y.at[p, 0], ey_s.at[p, 0],
                   ey_r.at[p, 0], {"gy": y_next}),
            remote(field.at[p, 0:8, :], halo_y.at[p, 1], ey_s.at[p, 1],
                   ey_r.at[p, 1], {"gy": y_prev}),
        ]
        for n, peer in enumerate(diagonals):
            zed, why = n // 2, n % 2
            copies.append(remote(edge_z.at[p, zed], corner.at[p, why, zed], ec_s.at[p, n],
                                 ec_r.at[p, n], peer))
        return copies

    def out_copy(p):
        return pltpu.make_async_copy(field.at[p], out.at[p // planes, p % planes], out_s.at[p])

    def send_edges(p):
        edge_z[p, 0] = jnp.transpose(field[p, :, width - 128 :])[120:128]
        edge_z[p, 1] = jnp.transpose(field[p, :, 0:128])[0:8]
        for copy in edge_copies(p):
            copy.start()
        out_copy(p).start()

    def prepare(p):
        for copy in edge_copies(p):
            copy.wait_recv()
        none = jnp.zeros((112, 128), F32)

        def unfold(low, high):
            return jnp.transpose(jnp.concatenate([low, high, none], axis=0))

        def put(rows, lanes, value):
            high, low = split(value)
            fboth[rows, lanes] = high
            fboth[rows.start + body : rows.stop + body, lanes] = low

        main, edge = slice(0, rows_y), slice(rows_y, body)
        inner, outer = slice(0, width), slice(width, width + 128)
        put(main, inner, field[p])
        put(main, outer, unfold(halo_z[p, 0], halo_z[p, 1]))
        put(edge, inner, jnp.concatenate([halo_y[p, 0], halo_y[p, 1]], axis=0))
        low = unfold(corner[p, 0, 0], corner[p, 0, 1])[rows_y - 8 :]
        high = unfold(corner[p, 1, 0], corner[p, 1, 1])[0:8]
        put(edge, outer, jnp.concatenate([low, high], axis=0))

    def lanes_of(u):
        return pl.ds(pl.multiple_of(u * chunk, chunk), chunk)

    def first_cell(row, start, length, at):
        near = cells[row : row + 1, at] - (start - 2)
        near = jnp.where(near < 0, near + length, near)
        return jnp.where(near >= length, near - length, near) - 3

    def weigh(u):
        at = lanes_of(u)
        for x, weight in enumerate(spline_weights(offs[0:1, at])):
            wxs[x, :, at] = weight
        wy = spline_weights(offs[1:2, at])
        wz = spline_weights(offs[2:3, at])
        first_y = first_cell(0, gy * rows_y, gy_count * rows_y, at)
        first_z = first_cell(1, me * width, 8 * width, at)

        @pl.loop(0, width // 32)
        def _(tile):
            spot = lax.broadcasted_iota(jnp.int32, (32, chunk), 0) + tile * 32
            rows = pl.ds(pl.multiple_of(tile * 32, 32), 32)
            pzhi[rows, at], pzlo[rows, at] = split(dense(spot - first_z, wz))
        h = lax.broadcasted_iota(jnp.int32, (16, chunk), 0)
        spot = jnp.where(h < 8, h - 8, h + (width - 8))
        pzhi[width : width + 16, at], pzlo[width : width + 16, at] = split(
            dense(spot - first_z, wz))
        zero = jnp.zeros((112, chunk), BF16)
        pzhi[width + 16 :, at] = zero
        pzlo[width + 16 :, at] = zero

        @pl.loop(0, (rows_y + 16) // 16)
        def _(tile):
            spot = lax.broadcasted_iota(jnp.int32, (16, chunk), 0) + (tile * 16 - 8)
            rows = pl.ds(pl.multiple_of(tile * 16, 16), 16)
            py[rows, at] = dense(spot - first_y, wy)

    def interpolate(p, u):
        c, x = p // planes, p % planes
        at = lanes_of(u)
        both = dot(fboth[...], pzhi[:, at])
        field_z = both[0:body] + both[body:] + dot(fboth[0:body], pzlo[:, at])
        value = jnp.sum(field_z[0:rows_y] * py[8 : 8 + rows_y, at], axis=0, keepdims=True)
        ends = (field_z[rows_y : rows_y + 8] * py[0:8, at]
                + field_z[rows_y + 8 :] * py[8 + rows_y :, at])
        value = (value + jnp.sum(ends, axis=0, keepdims=True)) * wxs[x, :, at]
        slot = lax.broadcasted_iota(jnp.int32, (1, chunk), 1) + u * chunk
        vals[c, :, at] = vals[c, :, at] + jnp.where(slot < count_ref[0], value, 0.0)

    def finish():
        @pl.loop(0, pieces)
        def _(p):
            for copy in edge_copies(p):
                copy.wait_send()
            out_copy(p).wait()

    vals[...] = jnp.zeros(vals.shape, F32)

    @pl.when(jnp.logical_not(is_hub))
    def _():
        pl.semaphore_wait(barrier, 11)

        @pl.loop(0, DIRECT)
        def _(j):
            give(j, side, 0, hub_same).start()
            give(j, 1 - side, 1, hub_other).start()

        @pl.loop(DIRECT, chunks)
        def _(j):
            give(j, 1 - side, 1, leaf_other).start()

        give(DIRECT, side, 0, hub_same).start()
        give(DIRECT + 1, side, 0, hub_same).start()

        pl.loop(0, groups)(weigh)

        def pass_on(j):
            arrival(j, leaf_other % 4).wait_recv()
            relay(j).start()

            @pl.when(j + 2 < chunks)
            def _():
                give(j + 2, side, 0, hub_same).start()

        pl.loop(DIRECT, FIRST_RELAYS)(pass_on)

        @pl.loop(0, pieces)
        def _(p):
            @pl.when(p > 0)
            def _():
                @pl.loop(0, RELAYS)
                def _(n):
                    j = FIRST_RELAYS + (p - 1) * RELAYS + n

                    @pl.when(j < chunks)
                    def _():
                        pass_on(j)

            @pl.loop(0, SUB)
            def _(n):
                taken(p * SUB + n, side).wait_recv()
                taken(p * SUB + n, 1 - side).wait_recv()
            send_edges(p)
            prepare(p)

            @pl.loop(0, groups)
            def _(u):
                interpolate(p, u)

        @pl.loop(0, chunks)
        def _(j):
            give(j, side, 0, hub_same).wait_send()
            give(j, 1 - side, 1, hub_other).wait_send()

            @pl.when(j >= DIRECT)
            def _():
                relay(j).wait_send()
        finish()

    def first_stage(j):
        own(j).wait()
        arrival(j, leaf_same % 4).wait_recv()
        arrival(j, leaf_other % 4).wait_recv()
        arrival(j, hub_other % 4).wait_recv()
        root = math.sqrt(0.5)

        @pl.loop(0, lines // 16)
        def _(group):
            rows = pl.ds(pl.multiple_of(group * 16, 16), 16)
            for tile in range(width // 128):
                lanes = slice(tile * 128, tile * 128 + 128)
                items = []
                for i in range(4):
                    f = factor[half, i : i + 1, lanes]
                    items.append((xbuf[j, i, 0, rows, lanes] * f, xbuf[j, i, 1, rows, lanes] * f))
                (ar, ai), (br, bi), (cr, ci), (dr, di) = items
                turned = [(ar, ai), ((br - bi) * root, (br + bi) * root), (-ci, cr),
                          ((dr + di) * -root, (dr - di) * root)]
                even, odd = dft(items), dft(turned)
                for m in range(parts):
                    yr, yi = (odd if m % 2 else even)[m // 2]
                    c, s = tcos[half, m : m + 1, lanes], tsin[half, m : m + 1, lanes]
                    zr, zi = yr * c - yi * s, yr * s + yi * c
                    at = pl.ds(pl.multiple_of(m * lines + group * 16, 16), 16)
                    shifted = slice(width + tile * 128, width + tile * 128 + 128)
                    hi, lo = split(zr)
                    yhi[at, lanes] = hi
                    ylo[at, lanes] = lo
                    hi, lo = split(zi)
                    yhi[at, shifted] = hi
                    ylo[at, shifted] = lo

        def product(which):
            lanes = pl.ds(pl.multiple_of(which * wide, wide), wide)
            left = yhi[...]
            return dot(left, whi[:, lanes]) + dot(ylo[...], whi[:, lanes]) + dot(left, wlo[:, lanes])

        zsend[j] = product(1 - half)
        cross(j).start()
        zown[j % (LAG + 1)] = product(half)

    def second_stage(j):
        cross(j).wait_recv()
        mine = j % (LAG + 1)
        targets = []
        for target in range(4):
            lanes = slice(target * each, target * each + each)
            terms = []
            for m in range(parts):
                rows = slice(m * lines, m * lines + lines)
                terms.append(zown[mine, rows, lanes] + zrecv[j, rows, lanes])
            targets.append(jnp.concatenate(terms, axis=1))
        hi, lo = split(jnp.concatenate(targets, axis=0))
        both = dot(jnp.concatenate([hi, lo], axis=0), perm[...])
        for target in range(4):
            at, low = target * lines, (4 + target) * lines
            total[j, target] = both[at : at + lines] + both[low : low + lines]
        hand(j, 0, leaf_same).start()
        hand(j, 1, leaf_other).start()
        hand(j, 2, hub_other).start()
        kept(j).start()

    def finish_piece(p):
        @pl.loop(0, SUB)
        def _(n):
            kept(p * SUB + n).wait()
            taken(p * SUB + n, 1 - side).wait_recv()
        send_edges(p)

    def spread(step):
        p, turn = step // SUB, step % SUB

        @pl.when(turn == 0)
        def _():
            prepare(p)

        @pl.loop(0, share)
        def _(n):
            interpolate(p, turn * share + n)

    @pl.when(is_hub)
    def _():
        @pl.loop(0, chunks)
        def _(j):
            own(j).start()
        pl.semaphore_wait(barrier, 12)

        @pl.loop(0, AHEAD)
        def _(j):
            give(j, 1 - side, 0, hub_other).start()

        pl.loop(0, groups)(weigh)
        first_edge = SUB - 1 + LAG + 2
        first_step = first_edge + 2
        steps = chunks + LAG

        @pl.loop(0, steps)
        def _(t):
            @pl.when(t < chunks)
            def _():
                first_stage(t)

            @pl.when(t + AHEAD < chunks)
            def _():
                give(t + AHEAD, 1 - side, 0, hub_other).start()

            @pl.when(t >= LAG)
            def _():
                second_stage(t - LAG)

            @pl.when((t >= first_edge) & ((t - first_edge) % SUB == 0))
            def _():
                finish_piece((t - first_edge) // SUB)

            @pl.when(t >= first_step)
            def _():
                spread(t - first_step)

        done = (steps - 1 - first_edge) // SUB + 1

        @pl.loop(steps - first_step, done * SUB)
        def _(step):
            spread(step)

        @pl.loop(done, pieces)
        def _(p):
            finish_piece(p)

        @pl.loop(done * SUB, pieces * SUB)
        def _(step):
            spread(step)

        @pl.loop(0, chunks)
        def _(j):
            give(j, 1 - side, 0, hub_other).wait_send()
            cross(j).wait_send()
            hand(j, 0, leaf_same).wait_send()
            hand(j, 1, leaf_other).wait_send()
            hand(j, 2, hub_other).wait_send()
        finish()


def hub_program(spectrum, cells, offsets, counts, tables):
    components, _, planes, rows_y, width = spectrum.shape
    slots = cells.shape[1]
    lines = rows_y // (2 * SUB)
    pieces = components * planes
    chunks = pieces * SUB
    factor, tcos, tsin, whi, wlo, perm = tables
    sign = np.ones((2, 8, 1), np.float32)
    sign[1, 1::2] = -1.0
    factor = factor.reshape(2, 4, width)
    tcos, tsin = tcos[None] * sign, tsin[None] * sign
    dma = pltpu.SemaphoreType.DMA
    vmem = pl.BlockSpec(memory_space=pltpu.VMEM)
    out, values = pl.pallas_call(
        hub_kernel,
        out_shape=(jax.ShapeDtypeStruct((components, planes, rows_y, width), F32),
                   jax.ShapeDtypeStruct((components, 1, slots), F32)),
        in_specs=[pl.BlockSpec(memory_space=pl.ANY), pl.BlockSpec(memory_space=pltpu.SMEM)]
        + [vmem] * 8,
        out_specs=(pl.BlockSpec(memory_space=pl.ANY), vmem),
        scratch_shapes=[
            pltpu.VMEM((chunks, 4, 2, lines, width), F32),
            pltpu.VMEM((8 * lines, 2 * width), BF16),
            pltpu.VMEM((8 * lines, 2 * width), BF16),
            pltpu.VMEM((LAG + 1, 8 * lines, width // 2), F32),
            pltpu.VMEM((chunks, 8 * lines, width // 2), F32),
            pltpu.VMEM((chunks, 8 * lines, width // 2), F32),
            pltpu.VMEM((chunks, 4, lines, width), F32),
            pltpu.VMEM((pieces, rows_y, width), F32),
            pltpu.VMEM((pieces, 2, 8, 128), F32),
            pltpu.VMEM((pieces, 2, 8, 128), F32),
            pltpu.VMEM((pieces, 2, 8, width), F32),
            pltpu.VMEM((pieces, 2, 2, 8, 128), F32),
            pltpu.VMEM((2 * (rows_y + 16), width + 128), BF16),
            pltpu.VMEM((width + 128, slots), BF16),
            pltpu.VMEM((width + 128, slots), BF16),
            pltpu.VMEM((rows_y + 16, slots), F32),
            pltpu.VMEM((planes, 1, slots), F32),
            dma((chunks, 3)),
            dma((chunks, 4)),
            dma((chunks,)),
            dma((chunks,)),
            dma((chunks, 3)),
            dma((chunks, 2)),
            dma((chunks,)),
            dma((chunks,)),
        ] + [dma((pieces, 2))] * 4 + [dma((pieces, 4))] * 2 + [dma((pieces,))],
        compiler_params=pltpu.CompilerParams(
            collective_id=0, has_side_effects=True, vmem_limit_bytes=63 << 20),
    )(spectrum, counts, cells, offsets, factor, tcos, tsin, whi, wlo, perm)
    return out, values.reshape(components, slots)


def general_transform(real, imag):
    parts, lines, width = real.shape
    length = parts * width
    k = np.arange(length, dtype=np.float64)
    symbol = (4.0 + 2.0 * np.cos(k * (2.0 * math.pi / length))) / 6.0
    factor = (1.0 / (symbol * math.sqrt(length))).reshape(parts, 1, width).astype(np.float32)
    real, imag = real * factor, imag * factor
    highest = lax.Precision.HIGHEST

    def table(left, right, modulus):
        angle = (np.outer(np.arange(left), np.arange(right)) % modulus) * (2 * math.pi / modulus)
        return np.cos(angle).astype(np.float32), np.sin(angle).astype(np.float32)

    c, s = table(parts, parts, parts)
    first = functools.partial(jnp.einsum, "ilk,im->mlk", precision=highest)
    yr, yi = first(real, c) - first(imag, s), first(real, s) + first(imag, c)
    c, s = table(parts, width, length)
    c, s = c[:, None], s[:, None]
    zr, zi = yr * c - yi * s, yr * s + yi * c
    c, s = table(width, width, width)
    last = functools.partial(jnp.einsum, "mlk,kq->lqm", precision=highest)
    out = (last(zr, c) - last(zi, s)).reshape(lines, parts, width)
    return jnp.moveaxis(out, 1, 0)


def spline_weights(frac):
    cube = frac * frac * frac
    square = frac * frac
    first = (1.0 - frac) * (1.0 - frac) * (1.0 - frac) / 6.0
    second = (3.0 * cube - 6.0 * square + 4.0) / 6.0
    third = (-3.0 * cube + 3.0 * square + 3.0 * frac + 1.0) / 6.0
    fourth = cube / 6.0
    return [first, second, third, fourth]


def dense(distance, weights):
    total = jnp.zeros(distance.shape, F32)
    for tap in range(4):
        total = jnp.where(distance == tap, weights[tap], total)
    return total


def halo_place(rows, size, chunk):
    h = lax.broadcasted_iota(jnp.int32, (rows, chunk), 0)
    return jnp.where(h < 3, h - 3, jnp.where(h < 6, h + (size - 3), -1000000))


def point_kernel(planes, count_ref, near_ref, off_ref, main_ref, zh_ref, yh_ref, cor_ref,
                 out_ref, fhi, flo, whi, wlo, wy_ref):
    block, width = main_ref.shape[0] // 3, main_ref.shape[1]
    rows_y = block // planes
    chunk = near_ref.shape[1]
    body = 3 * block

    @pl.when(pl.program_id(0) == 0)
    def _():
        for c in range(3):
            @pl.loop(0, planes)
            def _(x):
                dst = pl.ds(pl.multiple_of(c * block + x * rows_y, rows_y), rows_y)
                hi, lo = split(main_ref[dst, :])
                fhi[dst, 0:width] = hi
                flo[dst, 0:width] = lo
                hi, lo = split(zh_ref[dst, :])
                fhi[dst, width:] = hi
                flo[dst, width:] = lo
        hi, lo = split(yh_ref[...])
        fhi[body:, 0:width] = hi
        flo[body:, 0:width] = lo
        hi, lo = split(cor_ref[...])
        fhi[body:, width:] = hi
        flo[body:, width:] = lo

    wx = spline_weights(off_ref[0:1, :])
    wy = spline_weights(off_ref[1:2, :])
    wz = spline_weights(off_ref[2:3, :])
    first_y = near_ref[0:1, :] - 1
    first_z = near_ref[1:2, :] - 1
    for tile in range(width // 128):
        place = lax.broadcasted_iota(jnp.int32, (128, chunk), 0) + tile * 128
        hi, lo = split(dense(place - first_z, wz))
        whi[tile * 128 : tile * 128 + 128, :] = hi
        wlo[tile * 128 : tile * 128 + 128, :] = lo
    hi, lo = split(dense(halo_place(128, width, chunk) - first_z, wz))
    whi[width:, :] = hi
    wlo[width:, :] = lo
    place = lax.broadcasted_iota(jnp.int32, (rows_y, chunk), 0)
    wy_ref[0:rows_y, :] = dense(place - first_y, wy)
    wy_ref[rows_y:, :] = dense(halo_place(8, rows_y, chunk) - first_y, wy)

    def layer(begin, rows):
        high = fhi[begin : begin + rows, :]
        return (dot(high, whi[...]) + dot(flo[begin : begin + rows, :], whi[...])
                + dot(high, wlo[...]))

    slot = lax.broadcasted_iota(jnp.int32, (1, chunk), 1) + pl.program_id(0) * chunk
    live = slot < count_ref[0]
    edge = layer(body, 3 * planes * 8)
    for c in range(3):
        inner = layer(c * block, block)
        value = jnp.zeros((1, chunk), F32)
        for x in range(planes):
            part = jnp.sum(inner[x * rows_y : (x + 1) * rows_y] * wy_ref[0:rows_y, :], axis=0,
                           keepdims=True)
            at = (c * planes + x) * 8
            part = part + jnp.sum(edge[at : at + 8] * wy_ref[rows_y:, :], axis=0, keepdims=True)
            value = value + part * wx[x]
        out_ref[c : c + 1, :] = jnp.where(live, value, 0.0)


def sample(counts, near, offsets, main, zh, yh, cor, planes):
    slots = near.shape[1]
    block, width = main.shape[0] // 3, main.shape[1]
    rows_y = block // planes
    chunk = math.gcd(slots, 256)
    whole = pl.BlockSpec(memory_space=pltpu.VMEM)
    return pl.pallas_call(
        functools.partial(point_kernel, planes),
        out_shape=jax.ShapeDtypeStruct((3, slots), F32),
        grid=(slots // chunk,),
        in_specs=[
            pl.BlockSpec(memory_space=pltpu.SMEM),
            pl.BlockSpec((2, chunk), lambda i: (0, i)),
            pl.BlockSpec((3, chunk), lambda i: (0, i)),
        ] + [whole] * 4,
        out_specs=pl.BlockSpec((3, chunk), lambda i: (0, i)),
        scratch_shapes=[
            pltpu.VMEM((3 * block + 24 * planes, width + 128), BF16),
            pltpu.VMEM((3 * block + 24 * planes, width + 128), BF16),
            pltpu.VMEM((width + 128, chunk), BF16),
            pltpu.VMEM((width + 128, chunk), BF16),
            pltpu.VMEM((rows_y + 8, chunk), F32),
        ],
        compiler_params=pltpu.CompilerParams(vmem_limit_bytes=32 << 20),
    )(counts, near, offsets, main, zh, yh, cor)


def ring(axis):
    count = lax.axis_size(axis)
    forward = [(i, (i + 1) % count) for i in range(count)]
    return forward, [(b, a) for a, b in forward]


def per_device(spectrum, cells, offsets, counts):
    components, halves, planes, rows_y, rows_z = spectrum.shape
    parts = lax.axis_size("gz")
    length_z = rows_z * parts
    length_y = rows_y * lax.axis_size("gy")
    z_start = lax.axis_index("gz") * rows_z
    y_start = lax.axis_index("gy") * rows_y
    lines = planes * rows_y // parts
    tiled = rows_z % (parts * 64) == 0 and lines % 16 == 0
    tables = line_tables(parts, rows_z) if tiled else None
    exchange = functools.partial(
        lax.all_to_all, axis_name="gz", split_axis=0, concat_axis=0, tiled=True)
    if (parts == 8 and tiled and rows_y == 128 and planes == 4 and lax.axis_size("gy") > 2
            and cells.shape[1] % (256 * SUB) == 0):
        return hub_program(spectrum, cells, offsets, counts, tables)
    blocks = []
    for c in range(components):
        real = exchange(spectrum[c, 0].reshape(parts, lines, rows_z))
        imag = exchange(spectrum[c, 1].reshape(parts, lines, rows_z))
        done = transform(real, imag, tables) if tiled else general_transform(real, imag)
        blocks.append(exchange(done).reshape(planes, rows_y, rows_z))
    coefficients = jnp.stack(blocks)
    pieces = components * planes
    field = coefficients.reshape(pieces, rows_y, rows_z)

    forward, backward = ring("gz")
    flat_low = jnp.swapaxes(field[:, :, rows_z - 3 :], 1, 2)
    flat_high = jnp.swapaxes(field[:, :, :3], 1, 2)
    z_halo = jnp.concatenate(
        [lax.ppermute(flat_low, "gz", forward), lax.ppermute(flat_high, "gz", backward)], axis=1)
    forward, backward = ring("gy")
    y_low = lax.ppermute(field[:, rows_y - 3 :], "gy", forward)
    y_high = lax.ppermute(field[:, :3], "gy", backward)
    c_low = lax.ppermute(z_halo[:, :, rows_y - 3 :], "gy", forward)
    c_high = lax.ppermute(z_halo[:, :, :3], "gy", backward)
    y_halo = jnp.concatenate([y_low, y_high, jnp.zeros((pieces, 2, rows_z), F32)], axis=1)
    corner = jnp.concatenate([c_low, c_high, jnp.zeros((pieces, 6, 2), F32)], axis=2)

    def wide(item):
        item = jnp.swapaxes(item, 1, 2)
        return jnp.pad(item, ((0, 0), (0, 0), (0, 122))).reshape(-1, 128)

    near_y = (cells[0] - y_start + 2) % length_y - 2
    near_z = (cells[1] - z_start + 2) % length_z - 2
    interpolated = sample(
        counts, jnp.stack([near_y, near_z]), offsets,
        field.reshape(pieces * rows_y, rows_z),
        wide(z_halo), y_halo.reshape(pieces * 8, rows_z), wide(corner), planes)
    return (coefficients, interpolated)


def solution(mesh):
    placed = (
        P(None, None, None, "gy", "gz"),
        P(None, ("gz", "gy")),
        P(None, ("gz", "gy")),
        P(("gz", "gy")),
    )
    return jax.shard_map(
        per_device,
        mesh=mesh,
        in_specs=placed,
        out_specs=(P(None, None, "gy", "gz"), P(None, ("gz", "gy"))),
        check_vma=False,
    )
```

```python
import functools
import math

import jax
import jax.numpy as jnp
import numpy as np
from jax import lax
from jax.experimental import pallas as pl
from jax.experimental.pallas import tpu as pltpu
from jax.sharding import PartitionSpec as P

F32 = jnp.float32
BF16 = jnp.bfloat16


def split(value):
    high = value.astype(BF16)
    return high, (value - high.astype(F32)).astype(BF16)


def split_table(table):
    high = np.asarray(table, np.float32).astype(BF16)
    low = (table - high.astype(np.float64)).astype(np.float32).astype(BF16)
    return high, low


def dot(left, right):
    return jnp.dot(left, right, preferred_element_type=F32)


def dft(items):
    count = len(items)
    if count == 1:
        return items
    even = dft(items[0::2])
    odd = dft(items[1::2])
    half = count // 2
    low, high = [], []
    for m in range(half):
        er, ei = even[m]
        xr, xi = odd[m]
        if m == 0:
            tr, ti = xr, xi
        elif 4 * m == count:
            tr, ti = -xi, xr
        elif 8 * m == count:
            s = math.sqrt(0.5)
            tr, ti = (xr - xi) * s, (xr + xi) * s
        elif 8 * m == 3 * count:
            s = math.sqrt(0.5)
            tr, ti = (xr + xi) * -s, (xr - xi) * s
        else:
            c, s = math.cos(2 * math.pi * m / count), math.sin(2 * math.pi * m / count)
            tr, ti = xr * c - xi * s, xr * s + xi * c
        low.append((er + tr, ei + ti))
        high.append((er - tr, ei - ti))
    return low + high


def line_kernel(re_ref, im_ref, factor_ref, tcos_ref, tsin_ref, whi_ref, wlo_ref, perm_ref,
                out_ref, yhi_ref, ylo_ref, z_ref):
    parts, lines, width = re_ref.shape
    step = 16

    @pl.loop(0, lines // step)
    def _(group):
        rows = pl.ds(pl.multiple_of(group * step, step), step)
        for tile in range(width // 128):
            lanes = slice(tile * 128, tile * 128 + 128)
            items = []
            for i in range(parts):
                f = factor_ref[i : i + 1, lanes]
                items.append((re_ref[i, rows, lanes] * f, im_ref[i, rows, lanes] * f))
            for m, (yr, yi) in enumerate(dft(items)):
                c, s = tcos_ref[m : m + 1, lanes], tsin_ref[m : m + 1, lanes]
                zr, zi = yr * c - yi * s, yr * s + yi * c
                shifted = slice(width + tile * 128, width + tile * 128 + 128)
                hi, lo = split(zr)
                yhi_ref[m, rows, lanes] = hi
                ylo_ref[m, rows, lanes] = lo
                hi, lo = split(zi)
                yhi_ref[m, rows, shifted] = hi
                ylo_ref[m, rows, shifted] = lo

    @pl.loop(0, parts)
    def _(m):
        yhi = yhi_ref[m]
        z_ref[m] = dot(yhi, whi_ref[...]) + dot(ylo_ref[m], whi_ref[...]) + dot(yhi, wlo_ref[...])

    each = width // parts
    for target in range(parts):
        lanes = slice(target * each, target * each + each)
        joined = jnp.concatenate([z_ref[m, :, lanes] for m in range(parts)], axis=1)
        hi, lo = split(joined)
        out_ref[target] = dot(hi, perm_ref[...]) + dot(lo, perm_ref[...])


def transform(real, imag, tables):
    parts, lines, width = real.shape
    return pl.pallas_call(
        line_kernel,
        out_shape=jax.ShapeDtypeStruct((parts, lines, width), F32),
        in_specs=[pl.BlockSpec(memory_space=pltpu.VMEM)] * 8,
        out_specs=pl.BlockSpec(memory_space=pltpu.VMEM),
        scratch_shapes=[
            pltpu.VMEM((parts, lines, 2 * width), BF16),
            pltpu.VMEM((parts, lines, 2 * width), BF16),
            pltpu.VMEM((parts, lines, width), F32),
        ],
        compiler_params=pltpu.CompilerParams(vmem_limit_bytes=24 << 20),
        cost_estimate=pl.CostEstimate(
            flops=20 * parts * lines * width * width, bytes_accessed=12 * parts * lines * width,
            transcendentals=0),
    )(real, imag, *tables)


def line_tables(parts, width):
    length = parts * width
    k = np.arange(length, dtype=np.float64)
    symbol = (4.0 + 2.0 * np.cos(k * (2.0 * math.pi / length))) / 6.0
    factor = (1.0 / (symbol * math.sqrt(length))).reshape(parts, width).astype(np.float32)
    turn = np.outer(np.arange(parts), np.arange(width)) * (2.0 * math.pi / length)
    angle = (np.outer(np.arange(width), np.arange(width)) % width) * (2.0 * math.pi / width)
    whi, wlo = split_table(np.concatenate([np.cos(angle), -np.sin(angle)], axis=0))
    each = width // parts
    perm = np.zeros((width, width), np.float32)
    for m in range(parts):
        for q in range(each):
            perm[m * each + q, parts * q + m] = 1.0
    made = (factor, np.cos(turn).astype(np.float32), np.sin(turn).astype(np.float32),
            whi, wlo, perm.astype(BF16))
    return made


MESH = pl.DeviceIdType.MESH


SUB = 4
DIRECT = 2
AHEAD = 2
EARLY = 6
LAG = 2
DEPTH = 2


def hub_kernel(spec, count_ref, cells, offs, factor, tcos, tsin, whi, wlo, perm, out, vals,
               xbuf, yhi, ylo, zown, zsend, zrecv, total, field, edge_z, halo_z, halo_y, corner,
               fboth, pzhi, pzlo, py, wxs,
               send_a, recv_a, cross_s, cross_r, dist_s, dist_r, loc, keep,
               ez_s, ez_r, ey_s, ey_r, ec_s, ec_r, out_s):
    components, _, planes, rows_y, width = spec.shape
    lines = rows_y // (2 * SUB)
    pieces = components * planes
    chunks = pieces * SUB
    slots = cells.shape[1]
    chunk = 256
    groups = slots // chunk
    share = groups // SUB
    parts = 8
    each = width // parts
    wide = width // 2
    body = rows_y + 16
    me = lax.axis_index("gz")
    half = me // 4
    side = me % 2
    is_hub = ((me // 2) == 1) | ((me // 2) == 2)
    hub_same = 2 + 2 * half + side
    hub_other = 2 + 2 * half + (1 - side)
    leaf_same = 6 * half + side
    leaf_other = 6 * half + (1 - side)
    partner = 4 - 2 * half + side
    z_next, z_prev = lax.rem(me + 1, 8), lax.rem(me + 7, 8)
    gy, gy_count = lax.axis_index("gy"), lax.axis_size("gy")
    y_next, y_prev = lax.rem(gy + 1, gy_count), lax.rem(gy + gy_count - 1, gy_count)
    diagonals = [{"gz": z, "gy": y} for z in (z_next, z_prev) for y in (y_next, y_prev)]

    barrier = pltpu.get_barrier_semaphore()

    def greet(peer):
        pl.semaphore_signal(barrier, inc=1, device_id=peer, device_id_type=MESH)

    for peer in [{"gz": z_next}, {"gz": z_prev}, {"gy": y_next}, {"gy": y_prev}] + diagonals:
        greet(peer)

    @pl.when(is_hub)
    def _():
        for peer in (leaf_same, leaf_other, hub_other, partner):
            greet({"gz": peer})

    @pl.when(jnp.logical_not(is_hub))
    def _():
        for peer in (hub_same, hub_other, leaf_other):
            greet({"gz": peer})

    def rows_of(j, which):
        return pl.ds(pl.multiple_of(which * (lines * SUB) + (j % SUB) * lines, lines), lines)

    def remote(source, target, send, recv, peer):
        return pltpu.make_async_remote_copy(
            src_ref=source, dst_ref=target, send_sem=send, recv_sem=recv,
            device_id=peer if isinstance(peer, dict) else {"gz": peer}, device_id_type=MESH)

    def source(j, which):
        piece = j // SUB
        return spec.at[piece // planes, :, piece % planes, rows_of(j, which), :]

    def give(j, which, n, peer):
        return remote(source(j, which),
                      xbuf.at[j, me % 4], send_a.at[j, n], recv_a.at[j, me % 4], peer)

    def relay(j):
        slot = leaf_other % 4
        return remote(xbuf.at[j, slot], xbuf.at[j, slot], send_a.at[j, 2], recv_a.at[j, slot],
                      hub_same)

    def arrival(j, slot):
        return remote(xbuf.at[j, slot], xbuf.at[j, slot], send_a.at[j, 0], recv_a.at[j, slot],
                      partner)

    def own(j):
        return pltpu.make_async_copy(source(j, side),
                                     xbuf.at[j, me % 4], loc.at[j])

    def cross(j):
        return remote(zsend.at[j], zrecv.at[j], cross_s.at[j], cross_r.at[j], partner)

    def place(j, which):
        return field.at[j // SUB, rows_of(j, which), :]

    def hand(j, n, peer):
        return remote(total.at[j, peer % 4], place(j, side), dist_s.at[j, n],
                      dist_r.at[j, side], peer)

    def taken(j, which):
        return remote(total.at[j, 0], place(j, which), dist_s.at[j, 0], dist_r.at[j, which],
                      hub_other)

    def kept(j):
        return pltpu.make_async_copy(total.at[j, me % 4], place(j, side), keep.at[j])

    def edge_copies(p):
        copies = [
            remote(edge_z.at[p, 0], halo_z.at[p, 0], ez_s.at[p, 0], ez_r.at[p, 0], z_next),
            remote(edge_z.at[p, 1], halo_z.at[p, 1], ez_s.at[p, 1], ez_r.at[p, 1], z_prev),
            remote(field.at[p, rows_y - 8 :, :], halo_y.at[p, 0], ey_s.at[p, 0],
                   ey_r.at[p, 0], {"gy": y_next}),
            remote(field.at[p, 0:8, :], halo_y.at[p, 1], ey_s.at[p, 1],
                   ey_r.at[p, 1], {"gy": y_prev}),
        ]
        for n, peer in enumerate(diagonals):
            zed, why = n // 2, n % 2
            copies.append(remote(edge_z.at[p, zed], corner.at[p, why, zed], ec_s.at[p, n],
                                 ec_r.at[p, n], peer))
        return copies

    def out_copy(p):
        return pltpu.make_async_copy(field.at[p], out.at[p // planes, p % planes], out_s.at[p])

    def send_edges(p):
        edge_z[p, 0] = jnp.transpose(field[p, :, width - 128 :])[120:128]
        edge_z[p, 1] = jnp.transpose(field[p, :, 0:128])[0:8]
        for copy in edge_copies(p):
            copy.start()
        out_copy(p).start()

    def prepare(p):
        for copy in edge_copies(p):
            copy.wait_recv()
        none = jnp.zeros((112, 128), F32)

        def unfold(low, high):
            return jnp.transpose(jnp.concatenate([low, high, none], axis=0))

        def put(rows, lanes, value):
            high, low = split(value)
            fboth[rows, lanes] = high
            fboth[rows.start + body : rows.stop + body, lanes] = low

        main, edge = slice(0, rows_y), slice(rows_y, body)
        inner, outer = slice(0, width), slice(width, width + 128)
        put(main, inner, field[p])
        put(main, outer, unfold(halo_z[p, 0], halo_z[p, 1]))
        put(edge, inner, jnp.concatenate([halo_y[p, 0], halo_y[p, 1]], axis=0))
        low = unfold(corner[p, 0, 0], corner[p, 0, 1])[rows_y - 8 :]
        high = unfold(corner[p, 1, 0], corner[p, 1, 1])[0:8]
        put(edge, outer, jnp.concatenate([low, high], axis=0))

    def lanes_of(u):
        return pl.ds(pl.multiple_of(u * chunk, chunk), chunk)

    def first_cell(row, start, length, at):
        near = cells[row : row + 1, at] - (start - 2)
        near = jnp.where(near < 0, near + length, near)
        return jnp.where(near >= length, near - length, near) - 3

    def weigh(u):
        at = lanes_of(u)
        for x, weight in enumerate(spline_weights(offs[0:1, at])):
            wxs[x, :, at] = weight
        wy = spline_weights(offs[1:2, at])
        wz = spline_weights(offs[2:3, at])
        first_y = first_cell(0, gy * rows_y, gy_count * rows_y, at)
        first_z = first_cell(1, me * width, 8 * width, at)

        @pl.loop(0, width // 32)
        def _(tile):
            spot = lax.broadcasted_iota(jnp.int32, (32, chunk), 0) + tile * 32
            rows = pl.ds(pl.multiple_of(tile * 32, 32), 32)
            pzhi[rows, at], pzlo[rows, at] = split(dense(spot - first_z, wz))
        h = lax.broadcasted_iota(jnp.int32, (16, chunk), 0)
        spot = jnp.where(h < 8, h - 8, h + (width - 8))
        pzhi[width : width + 16, at], pzlo[width : width + 16, at] = split(
            dense(spot - first_z, wz))
        zero = jnp.zeros((112, chunk), BF16)
        pzhi[width + 16 :, at] = zero
        pzlo[width + 16 :, at] = zero

        @pl.loop(0, (rows_y + 16) // 16)
        def _(tile):
            spot = lax.broadcasted_iota(jnp.int32, (16, chunk), 0) + (tile * 16 - 8)
            rows = pl.ds(pl.multiple_of(tile * 16, 16), 16)
            py[rows, at] = dense(spot - first_y, wy)

    def interpolate(p, u):
        c, x = p // planes, p % planes
        at = lanes_of(u)
        both = dot(fboth[...], pzhi[:, at])
        field_z = both[0:body] + both[body:] + dot(fboth[0:body], pzlo[:, at])
        value = jnp.sum(field_z[0:rows_y] * py[8 : 8 + rows_y, at], axis=0, keepdims=True)
        ends = (field_z[rows_y : rows_y + 8] * py[0:8, at]
                + field_z[rows_y + 8 :] * py[8 + rows_y :, at])
        value = (value + jnp.sum(ends, axis=0, keepdims=True)) * wxs[x, :, at]
        slot = lax.broadcasted_iota(jnp.int32, (1, chunk), 1) + u * chunk
        vals[c, :, at] = vals[c, :, at] + jnp.where(slot < count_ref[0], value, 0.0)

    def finish():
        @pl.loop(0, pieces)
        def _(p):
            for copy in edge_copies(p):
                copy.wait_send()
            out_copy(p).wait()

    def spread(step):
        p, turn = step // SUB, step % SUB

        @pl.when(turn == 0)
        def _():
            prepare(p)

        @pl.loop(0, share)
        def _(n):
            interpolate(p, turn * share + n)

    vals[...] = jnp.zeros(vals.shape, F32)

    @pl.when(is_hub)
    def _():
        @pl.loop(0, chunks)
        def _(j):
            own(j).start()

    pl.loop(0, groups)(weigh)

    @pl.when(jnp.logical_not(is_hub))
    def _():
        pl.semaphore_wait(barrier, 11)

        @pl.loop(DIRECT, EARLY)
        def _(j):
            give(j, 1 - side, 1, leaf_other).start()

        first_edge = SUB - 1 + LAG + DEPTH + 4
        first_step = first_edge + 3

        def same(j):
            return give(j, side, 0, hub_same)

        def sent(j):
            same(j).wait_send()
            give(j, 1 - side, 1, hub_other).wait_send()

            @pl.when(j >= DIRECT)
            def _():
                relay(j).wait_send()

        def pass_on(j):
            @pl.when(j >= DEPTH)
            def _():
                sent(j - DEPTH)

            same(j).start()

            @pl.when(j + EARLY < chunks)
            def _():
                give(j + EARLY, 1 - side, 1, leaf_other).start()

            @pl.when(j < DIRECT)
            def _():
                give(j, 1 - side, 1, hub_other).start()

            @pl.when(j >= DIRECT)
            def _():
                arrival(j, leaf_other % 4).wait_recv()
                relay(j).start()

        def finish_piece(p):
            @pl.loop(0, SUB)
            def _(n):
                taken(p * SUB + n, side).wait_recv()
                taken(p * SUB + n, 1 - side).wait_recv()
            send_edges(p)

        steps = (pieces - 1) * SUB + first_edge + 1

        @pl.loop(0, steps)
        def _(t):
            @pl.when(t < chunks)
            def _():
                pass_on(t)

            @pl.when((t >= first_edge) & ((t - first_edge) % SUB == 0))
            def _():
                finish_piece((t - first_edge) // SUB)

            @pl.when(t >= first_step)
            def _():
                spread(t - first_step)

        @pl.loop(steps - first_step, chunks)
        def _(step):
            spread(step)

        @pl.loop(chunks - DEPTH, chunks)
        def _(j):
            sent(j)
        finish()

    def first_stage(j):
        own(j).wait()
        arrival(j, leaf_same % 4).wait_recv()
        arrival(j, leaf_other % 4).wait_recv()
        arrival(j, hub_other % 4).wait_recv()
        root = math.sqrt(0.5)

        @pl.loop(0, lines // 16)
        def _(group):
            rows = pl.ds(pl.multiple_of(group * 16, 16), 16)
            for tile in range(width // 128):
                lanes = slice(tile * 128, tile * 128 + 128)
                items = []
                for i in range(4):
                    f = factor[half, i : i + 1, lanes]
                    items.append((xbuf[j, i, 0, rows, lanes] * f, xbuf[j, i, 1, rows, lanes] * f))
                (ar, ai), (br, bi), (cr, ci), (dr, di) = items
                turned = [(ar, ai), ((br - bi) * root, (br + bi) * root), (-ci, cr),
                          ((dr + di) * -root, (dr - di) * root)]
                even, odd = dft(items), dft(turned)
                for m in range(parts):
                    yr, yi = (odd if m % 2 else even)[m // 2]
                    c, s = tcos[half, m : m + 1, lanes], tsin[half, m : m + 1, lanes]
                    zr, zi = yr * c - yi * s, yr * s + yi * c
                    at = pl.ds(pl.multiple_of(m * lines + group * 16, 16), 16)
                    shifted = slice(width + tile * 128, width + tile * 128 + 128)
                    hi, lo = split(zr)
                    yhi[at, lanes] = hi
                    ylo[at, lanes] = lo
                    hi, lo = split(zi)
                    yhi[at, shifted] = hi
                    ylo[at, shifted] = lo

        def product(which):
            lanes = pl.ds(pl.multiple_of(which * wide, wide), wide)
            left = yhi[...]
            return dot(left, whi[:, lanes]) + dot(ylo[...], whi[:, lanes]) + dot(left, wlo[:, lanes])

        zsend[j] = product(1 - half)
        cross(j).start()
        zown[j % (LAG + 1)] = product(half)

    def second_stage(j):
        cross(j).wait_recv()
        mine = j % (LAG + 1)
        targets = []
        for target in range(4):
            lanes = slice(target * each, target * each + each)
            terms = []
            for m in range(parts):
                rows = slice(m * lines, m * lines + lines)
                terms.append(zown[mine, rows, lanes] + zrecv[j, rows, lanes])
            targets.append(jnp.concatenate(terms, axis=1))
        hi, lo = split(jnp.concatenate(targets, axis=0))
        both = dot(jnp.concatenate([hi, lo], axis=0), perm[...])
        for target in range(4):
            at, low = target * lines, (4 + target) * lines
            total[j, target] = both[at : at + lines] + both[low : low + lines]
        hand(j, 0, leaf_same).start()
        hand(j, 1, leaf_other).start()
        hand(j, 2, hub_other).start()
        kept(j).start()

    def finish_piece(p):
        @pl.loop(0, SUB)
        def _(n):
            kept(p * SUB + n).wait()
            taken(p * SUB + n, 1 - side).wait_recv()
        send_edges(p)

    @pl.when(is_hub)
    def _():
        pl.semaphore_wait(barrier, 12)

        @pl.loop(0, AHEAD)
        def _(j):
            give(j, 1 - side, 0, hub_other).start()

        first_edge = SUB - 1 + LAG + 2
        first_step = first_edge + 5
        steps = chunks + LAG

        @pl.loop(0, steps)
        def _(t):
            @pl.when(t < chunks)
            def _():
                first_stage(t)

            @pl.when(t + AHEAD < chunks)
            def _():
                give(t + AHEAD, 1 - side, 0, hub_other).start()

            @pl.when(t >= LAG)
            def _():
                second_stage(t - LAG)

            @pl.when((t >= first_edge) & ((t - first_edge) % SUB == 0))
            def _():
                finish_piece((t - first_edge) // SUB)

            @pl.when(t >= first_step)
            def _():
                spread(t - first_step)

        done = (steps - 1 - first_edge) // SUB + 1

        @pl.loop(steps - first_step, (done - 1) * SUB)
        def _(step):
            spread(step)

        @pl.loop(done, pieces)
        def _(p):
            finish_piece(p)

        @pl.loop((done - 1) * SUB, chunks)
        def _(step):
            spread(step)

        @pl.loop(0, chunks)
        def _(j):
            give(j, 1 - side, 0, hub_other).wait_send()
            cross(j).wait_send()
            hand(j, 0, leaf_same).wait_send()
            hand(j, 1, leaf_other).wait_send()
            hand(j, 2, hub_other).wait_send()
        finish()


def hub_program(spectrum, cells, offsets, counts, tables):
    components, _, planes, rows_y, width = spectrum.shape
    slots = cells.shape[1]
    lines = rows_y // (2 * SUB)
    pieces = components * planes
    chunks = pieces * SUB
    factor, tcos, tsin, whi, wlo, perm = tables
    sign = np.ones((2, 8, 1), np.float32)
    sign[1, 1::2] = -1.0
    factor = factor.reshape(2, 4, width)
    tcos, tsin = tcos[None] * sign, tsin[None] * sign
    dma = pltpu.SemaphoreType.DMA
    vmem = pl.BlockSpec(memory_space=pltpu.VMEM)
    out, values = pl.pallas_call(
        hub_kernel,
        out_shape=(jax.ShapeDtypeStruct((components, planes, rows_y, width), F32),
                   jax.ShapeDtypeStruct((components, 1, slots), F32)),
        in_specs=[pl.BlockSpec(memory_space=pl.ANY), pl.BlockSpec(memory_space=pltpu.SMEM)]
        + [vmem] * 8,
        out_specs=(pl.BlockSpec(memory_space=pl.ANY), vmem),
        scratch_shapes=[
            pltpu.VMEM((chunks, 4, 2, lines, width), F32),
            pltpu.VMEM((8 * lines, 2 * width), BF16),
            pltpu.VMEM((8 * lines, 2 * width), BF16),
            pltpu.VMEM((LAG + 1, 8 * lines, width // 2), F32),
            pltpu.VMEM((chunks, 8 * lines, width // 2), F32),
            pltpu.VMEM((chunks, 8 * lines, width // 2), F32),
            pltpu.VMEM((chunks, 4, lines, width), F32),
            pltpu.VMEM((pieces, rows_y, width), F32),
            pltpu.VMEM((pieces, 2, 8, 128), F32),
            pltpu.VMEM((pieces, 2, 8, 128), F32),
            pltpu.VMEM((pieces, 2, 8, width), F32),
            pltpu.VMEM((pieces, 2, 2, 8, 128), F32),
            pltpu.VMEM((2 * (rows_y + 16), width + 128), BF16),
            pltpu.VMEM((width + 128, slots), BF16),
            pltpu.VMEM((width + 128, slots), BF16),
            pltpu.VMEM((rows_y + 16, slots), F32),
            pltpu.VMEM((planes, 1, slots), F32),
            dma((chunks, 3)),
            dma((chunks, 4)),
            dma((chunks,)),
            dma((chunks,)),
            dma((chunks, 3)),
            dma((chunks, 2)),
            dma((chunks,)),
            dma((chunks,)),
        ] + [dma((pieces, 2))] * 4 + [dma((pieces, 4))] * 2 + [dma((pieces,))],
        compiler_params=pltpu.CompilerParams(
            collective_id=0, has_side_effects=True, vmem_limit_bytes=63 << 20),
    )(spectrum, counts, cells, offsets, factor, tcos, tsin, whi, wlo, perm)
    return out, values.reshape(components, slots)


def general_transform(real, imag):
    parts, lines, width = real.shape
    length = parts * width
    k = np.arange(length, dtype=np.float64)
    symbol = (4.0 + 2.0 * np.cos(k * (2.0 * math.pi / length))) / 6.0
    factor = (1.0 / (symbol * math.sqrt(length))).reshape(parts, 1, width).astype(np.float32)
    real, imag = real * factor, imag * factor
    highest = lax.Precision.HIGHEST

    def table(left, right, modulus):
        angle = (np.outer(np.arange(left), np.arange(right)) % modulus) * (2 * math.pi / modulus)
        return np.cos(angle).astype(np.float32), np.sin(angle).astype(np.float32)

    c, s = table(parts, parts, parts)
    first = functools.partial(jnp.einsum, "ilk,im->mlk", precision=highest)
    yr, yi = first(real, c) - first(imag, s), first(real, s) + first(imag, c)
    c, s = table(parts, width, length)
    c, s = c[:, None], s[:, None]
    zr, zi = yr * c - yi * s, yr * s + yi * c
    c, s = table(width, width, width)
    last = functools.partial(jnp.einsum, "mlk,kq->lqm", precision=highest)
    out = (last(zr, c) - last(zi, s)).reshape(lines, parts, width)
    return jnp.moveaxis(out, 1, 0)


def spline_weights(frac):
    cube = frac * frac * frac
    square = frac * frac
    first = (1.0 - frac) * (1.0 - frac) * (1.0 - frac) / 6.0
    second = (3.0 * cube - 6.0 * square + 4.0) / 6.0
    third = (-3.0 * cube + 3.0 * square + 3.0 * frac + 1.0) / 6.0
    fourth = cube / 6.0
    return [first, second, third, fourth]


def dense(distance, weights):
    total = jnp.zeros(distance.shape, F32)
    for tap in range(4):
        total = jnp.where(distance == tap, weights[tap], total)
    return total


def halo_place(rows, size, chunk):
    h = lax.broadcasted_iota(jnp.int32, (rows, chunk), 0)
    return jnp.where(h < 3, h - 3, jnp.where(h < 6, h + (size - 3), -1000000))


def point_kernel(planes, count_ref, near_ref, off_ref, main_ref, zh_ref, yh_ref, cor_ref,
                 out_ref, fhi, flo, whi, wlo, wy_ref):
    block, width = main_ref.shape[0] // 3, main_ref.shape[1]
    rows_y = block // planes
    chunk = near_ref.shape[1]
    body = 3 * block

    @pl.when(pl.program_id(0) == 0)
    def _():
        for c in range(3):
            @pl.loop(0, planes)
            def _(x):
                dst = pl.ds(pl.multiple_of(c * block + x * rows_y, rows_y), rows_y)
                hi, lo = split(main_ref[dst, :])
                fhi[dst, 0:width] = hi
                flo[dst, 0:width] = lo
                hi, lo = split(zh_ref[dst, :])
                fhi[dst, width:] = hi
                flo[dst, width:] = lo
        hi, lo = split(yh_ref[...])
        fhi[body:, 0:width] = hi
        flo[body:, 0:width] = lo
        hi, lo = split(cor_ref[...])
        fhi[body:, width:] = hi
        flo[body:, width:] = lo

    wx = spline_weights(off_ref[0:1, :])
    wy = spline_weights(off_ref[1:2, :])
    wz = spline_weights(off_ref[2:3, :])
    first_y = near_ref[0:1, :] - 1
    first_z = near_ref[1:2, :] - 1
    for tile in range(width // 128):
        place = lax.broadcasted_iota(jnp.int32, (128, chunk), 0) + tile * 128
        hi, lo = split(dense(place - first_z, wz))
        whi[tile * 128 : tile * 128 + 128, :] = hi
        wlo[tile * 128 : tile * 128 + 128, :] = lo
    hi, lo = split(dense(halo_place(128, width, chunk) - first_z, wz))
    whi[width:, :] = hi
    wlo[width:, :] = lo
    place = lax.broadcasted_iota(jnp.int32, (rows_y, chunk), 0)
    wy_ref[0:rows_y, :] = dense(place - first_y, wy)
    wy_ref[rows_y:, :] = dense(halo_place(8, rows_y, chunk) - first_y, wy)

    def layer(begin, rows):
        high = fhi[begin : begin + rows, :]
        return (dot(high, whi[...]) + dot(flo[begin : begin + rows, :], whi[...])
                + dot(high, wlo[...]))

    slot = lax.broadcasted_iota(jnp.int32, (1, chunk), 1) + pl.program_id(0) * chunk
    live = slot < count_ref[0]
    edge = layer(body, 3 * planes * 8)
    for c in range(3):
        inner = layer(c * block, block)
        value = jnp.zeros((1, chunk), F32)
        for x in range(planes):
            part = jnp.sum(inner[x * rows_y : (x + 1) * rows_y] * wy_ref[0:rows_y, :], axis=0,
                           keepdims=True)
            at = (c * planes + x) * 8
            part = part + jnp.sum(edge[at : at + 8] * wy_ref[rows_y:, :], axis=0, keepdims=True)
            value = value + part * wx[x]
        out_ref[c : c + 1, :] = jnp.where(live, value, 0.0)


def sample(counts, near, offsets, main, zh, yh, cor, planes):
    slots = near.shape[1]
    block, width = main.shape[0] // 3, main.shape[1]
    rows_y = block // planes
    chunk = math.gcd(slots, 256)
    whole = pl.BlockSpec(memory_space=pltpu.VMEM)
    return pl.pallas_call(
        functools.partial(point_kernel, planes),
        out_shape=jax.ShapeDtypeStruct((3, slots), F32),
        grid=(slots // chunk,),
        in_specs=[
            pl.BlockSpec(memory_space=pltpu.SMEM),
            pl.BlockSpec((2, chunk), lambda i: (0, i)),
            pl.BlockSpec((3, chunk), lambda i: (0, i)),
        ] + [whole] * 4,
        out_specs=pl.BlockSpec((3, chunk), lambda i: (0, i)),
        scratch_shapes=[
            pltpu.VMEM((3 * block + 24 * planes, width + 128), BF16),
            pltpu.VMEM((3 * block + 24 * planes, width + 128), BF16),
            pltpu.VMEM((width + 128, chunk), BF16),
            pltpu.VMEM((width + 128, chunk), BF16),
            pltpu.VMEM((rows_y + 8, chunk), F32),
        ],
        compiler_params=pltpu.CompilerParams(vmem_limit_bytes=32 << 20),
    )(counts, near, offsets, main, zh, yh, cor)


def ring(axis):
    count = lax.axis_size(axis)
    forward = [(i, (i + 1) % count) for i in range(count)]
    return forward, [(b, a) for a, b in forward]


def per_device(spectrum, cells, offsets, counts):
    components, halves, planes, rows_y, rows_z = spectrum.shape
    parts = lax.axis_size("gz")
    length_z = rows_z * parts
    length_y = rows_y * lax.axis_size("gy")
    z_start = lax.axis_index("gz") * rows_z
    y_start = lax.axis_index("gy") * rows_y
    lines = planes * rows_y // parts
    tiled = rows_z % (parts * 64) == 0 and lines % 16 == 0
    tables = line_tables(parts, rows_z) if tiled else None
    exchange = functools.partial(
        lax.all_to_all, axis_name="gz", split_axis=0, concat_axis=0, tiled=True)
    if (parts == 8 and tiled and rows_y == 128 and planes == 4 and lax.axis_size("gy") > 2
            and cells.shape[1] % (256 * SUB) == 0):
        return hub_program(spectrum, cells, offsets, counts, tables)
    blocks = []
    for c in range(components):
        real = exchange(spectrum[c, 0].reshape(parts, lines, rows_z))
        imag = exchange(spectrum[c, 1].reshape(parts, lines, rows_z))
        done = transform(real, imag, tables) if tiled else general_transform(real, imag)
        blocks.append(exchange(done).reshape(planes, rows_y, rows_z))
    coefficients = jnp.stack(blocks)
    pieces = components * planes
    field = coefficients.reshape(pieces, rows_y, rows_z)

    forward, backward = ring("gz")
    flat_low = jnp.swapaxes(field[:, :, rows_z - 3 :], 1, 2)
    flat_high = jnp.swapaxes(field[:, :, :3], 1, 2)
    z_halo = jnp.concatenate(
        [lax.ppermute(flat_low, "gz", forward), lax.ppermute(flat_high, "gz", backward)], axis=1)
    forward, backward = ring("gy")
    y_low = lax.ppermute(field[:, rows_y - 3 :], "gy", forward)
    y_high = lax.ppermute(field[:, :3], "gy", backward)
    c_low = lax.ppermute(z_halo[:, :, rows_y - 3 :], "gy", forward)
    c_high = lax.ppermute(z_halo[:, :, :3], "gy", backward)
    y_halo = jnp.concatenate([y_low, y_high, jnp.zeros((pieces, 2, rows_z), F32)], axis=1)
    corner = jnp.concatenate([c_low, c_high, jnp.zeros((pieces, 6, 2), F32)], axis=2)

    def wide(item):
        item = jnp.swapaxes(item, 1, 2)
        return jnp.pad(item, ((0, 0), (0, 0), (0, 122))).reshape(-1, 128)

    near_y = (cells[0] - y_start + 2) % length_y - 2
    near_z = (cells[1] - z_start + 2) % length_z - 2
    interpolated = sample(
        counts, jnp.stack([near_y, near_z]), offsets,
        field.reshape(pieces * rows_y, rows_z),
        wide(z_halo), y_halo.reshape(pieces * 8, rows_z), wide(corner), planes)
    return (coefficients, interpolated)


def solution(mesh):
    placed = (
        P(None, None, None, "gy", "gz"),
        P(None, ("gz", "gy")),
        P(None, ("gz", "gy")),
        P(("gz", "gy")),
    )
    return jax.shard_map(
        per_device,
        mesh=mesh,
        in_specs=placed,
        out_specs=(P(None, None, "gy", "gz"), P(None, ("gz", "gy"))),
        check_vma=False,
    )
```

```python
import functools
import math

import jax
import jax.numpy as jnp
import numpy as np
from jax import lax
from jax.experimental import pallas as pl
from jax.experimental.pallas import tpu as pltpu
from jax.sharding import PartitionSpec as P

F32 = jnp.float32
BF16 = jnp.bfloat16


def split(value):
    high = value.astype(BF16)
    return high, (value - high.astype(F32)).astype(BF16)


def split_table(table):
    high = np.asarray(table, np.float32).astype(BF16)
    low = (table - high.astype(np.float64)).astype(np.float32).astype(BF16)
    return high, low


def dot(left, right):
    return jnp.dot(left, right, preferred_element_type=F32)


def dft(items):
    count = len(items)
    if count == 1:
        return items
    even = dft(items[0::2])
    odd = dft(items[1::2])
    half = count // 2
    low, high = [], []
    for m in range(half):
        er, ei = even[m]
        xr, xi = odd[m]
        if m == 0:
            tr, ti = xr, xi
        elif 4 * m == count:
            tr, ti = -xi, xr
        elif 8 * m == count:
            s = math.sqrt(0.5)
            tr, ti = (xr - xi) * s, (xr + xi) * s
        elif 8 * m == 3 * count:
            s = math.sqrt(0.5)
            tr, ti = (xr + xi) * -s, (xr - xi) * s
        else:
            c, s = math.cos(2 * math.pi * m / count), math.sin(2 * math.pi * m / count)
            tr, ti = xr * c - xi * s, xr * s + xi * c
        low.append((er + tr, ei + ti))
        high.append((er - tr, ei - ti))
    return low + high


def line_kernel(re_ref, im_ref, factor_ref, tcos_ref, tsin_ref, whi_ref, wlo_ref, perm_ref,
                out_ref, yhi_ref, ylo_ref, z_ref):
    parts, lines, width = re_ref.shape
    step = 16

    @pl.loop(0, lines // step)
    def _(group):
        rows = pl.ds(pl.multiple_of(group * step, step), step)
        for tile in range(width // 128):
            lanes = slice(tile * 128, tile * 128 + 128)
            items = []
            for i in range(parts):
                f = factor_ref[i : i + 1, lanes]
                items.append((re_ref[i, rows, lanes] * f, im_ref[i, rows, lanes] * f))
            for m, (yr, yi) in enumerate(dft(items)):
                c, s = tcos_ref[m : m + 1, lanes], tsin_ref[m : m + 1, lanes]
                zr, zi = yr * c - yi * s, yr * s + yi * c
                shifted = slice(width + tile * 128, width + tile * 128 + 128)
                hi, lo = split(zr)
                yhi_ref[m, rows, lanes] = hi
                ylo_ref[m, rows, lanes] = lo
                hi, lo = split(zi)
                yhi_ref[m, rows, shifted] = hi
                ylo_ref[m, rows, shifted] = lo

    @pl.loop(0, parts)
    def _(m):
        yhi = yhi_ref[m]
        z_ref[m] = dot(yhi, whi_ref[...]) + dot(ylo_ref[m], whi_ref[...]) + dot(yhi, wlo_ref[...])

    each = width // parts
    for target in range(parts):
        lanes = slice(target * each, target * each + each)
        joined = jnp.concatenate([z_ref[m, :, lanes] for m in range(parts)], axis=1)
        hi, lo = split(joined)
        out_ref[target] = dot(hi, perm_ref[...]) + dot(lo, perm_ref[...])


def transform(real, imag, tables):
    parts, lines, width = real.shape
    return pl.pallas_call(
        line_kernel,
        out_shape=jax.ShapeDtypeStruct((parts, lines, width), F32),
        in_specs=[pl.BlockSpec(memory_space=pltpu.VMEM)] * 8,
        out_specs=pl.BlockSpec(memory_space=pltpu.VMEM),
        scratch_shapes=[
            pltpu.VMEM((parts, lines, 2 * width), BF16),
            pltpu.VMEM((parts, lines, 2 * width), BF16),
            pltpu.VMEM((parts, lines, width), F32),
        ],
        compiler_params=pltpu.CompilerParams(vmem_limit_bytes=24 << 20),
        cost_estimate=pl.CostEstimate(
            flops=20 * parts * lines * width * width, bytes_accessed=12 * parts * lines * width,
            transcendentals=0),
    )(real, imag, *tables)


def line_tables(parts, width):
    length = parts * width
    k = np.arange(length, dtype=np.float64)
    symbol = (4.0 + 2.0 * np.cos(k * (2.0 * math.pi / length))) / 6.0
    factor = (1.0 / (symbol * math.sqrt(length))).reshape(parts, width).astype(np.float32)
    turn = np.outer(np.arange(parts), np.arange(width)) * (2.0 * math.pi / length)
    angle = (np.outer(np.arange(width), np.arange(width)) % width) * (2.0 * math.pi / width)
    whi, wlo = split_table(np.concatenate([np.cos(angle), -np.sin(angle)], axis=0))
    each = width // parts
    perm = np.zeros((width, width), np.float32)
    for m in range(parts):
        for q in range(each):
            perm[m * each + q, parts * q + m] = 1.0
    made = (factor, np.cos(turn).astype(np.float32), np.sin(turn).astype(np.float32),
            whi, wlo, perm.astype(BF16))
    return made


MESH = pl.DeviceIdType.MESH


SUB = 4
DIRECT = 2
AHEAD = 2
EARLY = 6
LAG = 2
DEPTH = 2


def hub_kernel(spec, count_ref, cells, offs, factor, tcos, tsin, whi, wlo, perm, out, vals,
               xbuf, yhi, ylo, zown, zsend, zrecv, rim_out, rim_in, total, field, halo_y,
               fboth, pzhi, pzlo, py, wxs, acc,
               send_a, recv_a, cross_s, cross_r, rim_s, rim_r, dist_s, dist_r, loc, keep,
               halo_s, halo_r, out_s):
    components, _, planes, rows_y, width = spec.shape
    lines = rows_y // (2 * SUB)
    pieces = components * planes
    chunks = pieces * SUB
    slots = cells.shape[1]
    chunk = 256
    groups = slots // chunk
    share = groups // SUB
    parts = 8
    each = width // parts
    wide = width // 2
    body = rows_y + 16
    me = lax.axis_index("gz")
    half = me // 4
    side = me % 2
    is_hub = ((me // 2) == 1) | ((me // 2) == 2)
    hub_same = 2 + 2 * half + side
    hub_other = 2 + 2 * half + (1 - side)
    leaf_same = 6 * half + side
    leaf_other = 6 * half + (1 - side)
    partner = 4 - 2 * half + side
    gy, gy_count = lax.axis_index("gy"), lax.axis_size("gy")
    y_next, y_prev = lax.rem(gy + 1, gy_count), lax.rem(gy + gy_count - 1, gy_count)

    barrier = pltpu.get_barrier_semaphore()

    def greet(peer):
        pl.semaphore_signal(barrier, inc=1, device_id=peer, device_id_type=MESH)

    greet({"gz": 2 + 2 * half, "gy": y_next})
    greet({"gz": 3 + 2 * half, "gy": y_prev})

    @pl.when(is_hub)
    def _():
        for peer in (leaf_same, leaf_other, hub_other, partner):
            greet({"gz": peer})
        beside = jnp.where(side == 1, y_next, y_prev)
        for target in range(4):
            greet({"gz": 4 * half + target, "gy": beside})

    @pl.when(jnp.logical_not(is_hub))
    def _():
        for peer in (hub_same, hub_other, leaf_other):
            greet({"gz": peer})

    def rows_of(j, which):
        return pl.ds(pl.multiple_of(which * (lines * SUB) + (j % SUB) * lines, lines), lines)

    def remote(source, target, send, recv, peer):
        return pltpu.make_async_remote_copy(
            src_ref=source, dst_ref=target, send_sem=send, recv_sem=recv,
            device_id=peer if isinstance(peer, dict) else {"gz": peer}, device_id_type=MESH)

    def source(j, which):
        piece = j // SUB
        return spec.at[piece // planes, :, piece % planes, rows_of(j, which), :]

    def give(j, which, n, peer):
        return remote(source(j, which),
                      xbuf.at[j, me % 4], send_a.at[j, n], recv_a.at[j, me % 4], peer)

    def relay(j):
        slot = leaf_other % 4
        return remote(xbuf.at[j, slot], xbuf.at[j, slot], send_a.at[j, 2], recv_a.at[j, slot],
                      hub_same)

    def arrival(j, slot):
        return remote(xbuf.at[j, slot], xbuf.at[j, slot], send_a.at[j, 0], recv_a.at[j, slot],
                      partner)

    def own(j):
        return pltpu.make_async_copy(source(j, side),
                                     xbuf.at[j, me % 4], loc.at[j])

    def cross(j):
        return remote(zsend.at[j], zrecv.at[j], cross_s.at[j], cross_r.at[j], partner)

    def rim(j):
        return remote(rim_out.at[j], rim_in.at[j], rim_s.at[j], rim_r.at[j], partner)

    def place(j, which):
        return field.at[j // SUB, rows_of(j, which), :]

    def hand(j, n, peer):
        return remote(total.at[j, peer % 4], place(j, side), dist_s.at[j, n],
                      dist_r.at[j, side], peer)

    def taken(j, which):
        return remote(total.at[j, 0], place(j, which), dist_s.at[j, 0], dist_r.at[j, which],
                      hub_other)

    def kept(j):
        return pltpu.make_async_copy(total.at[j, me % 4], place(j, side), keep.at[j])

    def border(p, target, last):
        if last:
            rows, peer = total.at[p * SUB + SUB - 1, target, lines - 8 :, :], y_next
        else:
            rows, peer = total.at[p * SUB, target, 0:8, :], y_prev
        at = 0 if last else 1
        return remote(rows, halo_y.at[p, at], halo_s.at[p, target], halo_r.at[p, at],
                      {"gz": 4 * half + target, "gy": peer})

    def out_copy(p):
        return pltpu.make_async_copy(field.at[p, :, 0:width], out.at[p // planes, p % planes],
                                     out_s.at[p])

    def prepare(p):
        @pl.when(is_hub)
        def _():
            @pl.loop(0, SUB)
            def _(n):
                kept(p * SUB + n).wait()

        @pl.when(jnp.logical_not(is_hub))
        def _():
            @pl.loop(0, SUB)
            def _(n):
                taken(p * SUB + n, side).wait_recv()

        @pl.loop(0, SUB)
        def _(n):
            taken(p * SUB + n, 1 - side).wait_recv()
        out_copy(p).start()
        border(p, 0, True).wait_recv()
        border(p, 0, False).wait_recv()
        fboth[0:rows_y], fboth[body : body + rows_y] = split(field[p])
        fboth[rows_y:body], fboth[body + rows_y :] = split(
            jnp.concatenate([halo_y[p, 0], halo_y[p, 1]], axis=0))

    def lanes_of(u):
        return pl.ds(pl.multiple_of(u * chunk, chunk), chunk)

    def first_cell(row, start, length, at):
        near = cells[row : row + 1, at] - (start - 2)
        near = jnp.where(near < 0, near + length, near)
        return jnp.where(near >= length, near - length, near) - 3

    def weigh(u):
        at = lanes_of(u)
        for x, weight in enumerate(spline_weights(offs[0:1, at])):
            wxs[x, :, at] = weight
        wy = spline_weights(offs[1:2, at])
        wz = spline_weights(offs[2:3, at])
        first_y = first_cell(0, gy * rows_y, gy_count * rows_y, at)
        first_z = first_cell(1, me * width, 8 * width, at)

        @pl.loop(0, width // 32)
        def _(tile):
            spot = lax.broadcasted_iota(jnp.int32, (32, chunk), 0) + tile * 32
            rows = pl.ds(pl.multiple_of(tile * 32, 32), 32)
            pzhi[rows, at], pzlo[rows, at] = split(dense(spot - first_z, wz))
        h = lax.broadcasted_iota(jnp.int32, (16, chunk), 0)
        spot = jnp.where(h < 8, h - 8, h + (width - 8))
        pzhi[width : width + 16, at], pzlo[width : width + 16, at] = split(
            dense(spot - first_z, wz))
        zero = jnp.zeros((112, chunk), BF16)
        pzhi[width + 16 :, at] = zero
        pzlo[width + 16 :, at] = zero

        @pl.loop(0, (rows_y + 16) // 16)
        def _(tile):
            spot = lax.broadcasted_iota(jnp.int32, (16, chunk), 0) + (tile * 16 - 8)
            rows = pl.ds(pl.multiple_of(tile * 16, 16), 16)
            py[rows, at] = dense(spot - first_y, wy)

    def interpolate(p, u):
        c, x = p // planes, p % planes
        at = lanes_of(u)
        both = dot(fboth[...], pzhi[:, at])
        field_z = both[0:body] + both[body:] + dot(fboth[0:body], pzlo[:, at])
        value = jnp.sum(field_z[0:rows_y] * py[8 : 8 + rows_y, at], axis=0, keepdims=True)
        ends = (field_z[rows_y : rows_y + 8] * py[0:8, at]
                + field_z[rows_y + 8 :] * py[8 + rows_y :, at])
        value = (value + jnp.sum(ends, axis=0, keepdims=True)) * wxs[x, :, at]
        acc[c, :, at] = acc[c, :, at] + value

    def finish():
        slot = lax.broadcasted_iota(jnp.int32, (1, slots), 1)
        for c in range(components):
            vals[c : c + 1, :] = jnp.where(slot < count_ref[0], acc[c], 0.0)

        @pl.loop(0, pieces)
        def _(p):
            out_copy(p).wait()

    def spread(step):
        p, turn = step // SUB, step % SUB

        @pl.when(turn == 0)
        def _():
            prepare(p)

        @pl.loop(0, share)
        def _(n):
            interpolate(p, turn * share + n)

    acc[...] = jnp.zeros(acc.shape, F32)

    @pl.when(is_hub)
    def _():
        @pl.loop(0, chunks)
        def _(j):
            own(j).start()

    @pl.when(jnp.logical_not(is_hub))
    def _():
        pl.semaphore_wait(barrier, 5)

        @pl.loop(DIRECT, EARLY)
        def _(j):
            give(j, 1 - side, 1, leaf_other).start()

        first_step = SUB + LAG + DEPTH + 4

        def same(j):
            return give(j, side, 0, hub_same)

        def sent(j):
            same(j).wait_send()
            give(j, 1 - side, 1, hub_other).wait_send()

            @pl.when(j >= DIRECT)
            def _():
                relay(j).wait_send()

        def pass_on(j):
            @pl.when(j >= DEPTH)
            def _():
                sent(j - DEPTH)

            same(j).start()

            @pl.when(j + EARLY < chunks)
            def _():
                give(j + EARLY, 1 - side, 1, leaf_other).start()

            @pl.when(j < DIRECT)
            def _():
                give(j, 1 - side, 1, hub_other).start()

            @pl.when(j >= DIRECT)
            def _():
                arrival(j, leaf_other % 4).wait_recv()
                relay(j).start()

        @pl.loop(0, chunks + first_step)
        def _(t):
            @pl.when(t < chunks)
            def _():
                pass_on(t)

            @pl.when(t < groups)
            def _():
                weigh(t)

            @pl.when(t >= first_step)
            def _():
                spread(t - first_step)

        @pl.loop(chunks - DEPTH, chunks)
        def _(j):
            sent(j)
        finish()

    def first_stage(j):
        own(j).wait()
        arrival(j, leaf_same % 4).wait_recv()
        arrival(j, leaf_other % 4).wait_recv()
        arrival(j, hub_other % 4).wait_recv()
        root = math.sqrt(0.5)

        @pl.loop(0, lines // 16)
        def _(group):
            rows = pl.ds(pl.multiple_of(group * 16, 16), 16)
            for tile in range(width // 128):
                lanes = slice(tile * 128, tile * 128 + 128)
                items = []
                for i in range(4):
                    f = factor[half, i : i + 1, lanes]
                    items.append((xbuf[j, i, 0, rows, lanes] * f, xbuf[j, i, 1, rows, lanes] * f))
                (ar, ai), (br, bi), (cr, ci), (dr, di) = items
                turned = [(ar, ai), ((br - bi) * root, (br + bi) * root), (-ci, cr),
                          ((dr + di) * -root, (dr - di) * root)]
                even, odd = dft(items), dft(turned)
                for m in range(parts):
                    yr, yi = (odd if m % 2 else even)[m // 2]
                    c, s = tcos[half, m : m + 1, lanes], tsin[half, m : m + 1, lanes]
                    zr, zi = yr * c - yi * s, yr * s + yi * c
                    at = pl.ds(pl.multiple_of(m * lines + group * 16, 16), 16)
                    shifted = slice(width + tile * 128, width + tile * 128 + 128)
                    hi, lo = split(zr)
                    yhi[at, lanes] = hi
                    ylo[at, lanes] = lo
                    hi, lo = split(zi)
                    yhi[at, shifted] = hi
                    ylo[at, shifted] = lo

        def product(which):
            lanes = pl.ds(pl.multiple_of(which * wide, wide), wide)
            left = yhi[...]
            return dot(left, whi[:, lanes]) + dot(ylo[...], whi[:, lanes]) + dot(left, wlo[:, lanes])

        zsend[j] = product(1 - half)
        cross(j).start()
        kept_part = product(half)
        zown[j % (LAG + 1)] = kept_part
        rim_out[j] = jnp.concatenate([jnp.transpose(kept_part[:, wide - 128 :])[127:128],
                                      jnp.transpose(kept_part[:, 0:128])[0:1]], axis=0)
        rim(j).start()

    def second_stage(j):
        cross(j).wait_recv()
        rim(j).wait_recv()
        mine = j % (LAG + 1)
        targets = []
        for target in range(4):
            lanes = slice(target * each, target * each + each)
            terms = []
            for m in range(parts):
                rows = slice(m * lines, m * lines + lines)
                terms.append(zown[mine, rows, lanes] + zrecv[j, rows, lanes])
            targets.append(jnp.concatenate(terms, axis=1))
        count = parts * lines
        lane = lax.broadcasted_iota(jnp.int32, (count, 128), 1)
        theirs = jnp.transpose(jnp.concatenate([rim_in[j], jnp.zeros((126, count), F32)], axis=0))
        ends = theirs + jnp.where(
            lane == 0, pltpu.roll(zsend[j, :, wide - 128 :], 1, 1),
            jnp.where(lane == 1, pltpu.roll(zsend[j, :, 0:128], 1, 1), 0.0))
        targets.append(jnp.concatenate(
            [ends[m * lines : m * lines + lines, 0:each] for m in range(parts)], axis=1))
        hi, lo = split(jnp.concatenate(targets, axis=0))
        both = dot(jnp.concatenate([hi, lo], axis=0), perm[...])
        full = both[0 : 5 * lines] + both[5 * lines :]
        ends = full[4 * lines :, 0:128]
        lane = lax.broadcasted_iota(jnp.int32, (lines, 128), 1)
        for target in range(4):
            at = target * lines
            low = ends if target == 0 else pltpu.roll(full[at - lines : at, width - 128 :], 8, 1)
            high = ends if target == 3 else pltpu.roll(full[at + lines : at + 2 * lines, 0:128], 8, 1)
            total[j, target, :, 0:width] = full[at : at + lines]
            total[j, target, :, width:] = jnp.where(
                lane < 8, low, jnp.where(lane < 16, high, 0.0))
        hand(j, 0, leaf_same).start()
        hand(j, 1, leaf_other).start()
        hand(j, 2, hub_other).start()
        kept(j).start()

        @pl.when((side == 1) & (j % SUB == SUB - 1))
        def _():
            for target in range(4):
                border(j // SUB, target, True).start()

        @pl.when((side == 0) & (j % SUB == 0))
        def _():
            for target in range(4):
                border(j // SUB, target, False).start()

    @pl.when(is_hub)
    def _():
        pl.semaphore_wait(barrier, 10)

        @pl.loop(0, AHEAD)
        def _(j):
            give(j, 1 - side, 0, hub_other).start()

        first_step = SUB + LAG + 2
        steps = chunks + LAG

        @pl.loop(0, steps)
        def _(t):
            @pl.when(t < chunks)
            def _():
                first_stage(t)

            @pl.when(t + AHEAD < chunks)
            def _():
                give(t + AHEAD, 1 - side, 0, hub_other).start()

            @pl.when(t >= LAG)
            def _():
                second_stage(t - LAG)

            @pl.when(t < groups)
            def _():
                weigh(t)

            @pl.when(t >= first_step)
            def _():
                spread(t - first_step)

        @pl.loop(steps - first_step, chunks)
        def _(step):
            spread(step)

        @pl.loop(0, chunks)
        def _(j):
            give(j, 1 - side, 0, hub_other).wait_send()
            cross(j).wait_send()
            rim(j).wait_send()
            hand(j, 0, leaf_same).wait_send()
            hand(j, 1, leaf_other).wait_send()
            hand(j, 2, hub_other).wait_send()

        @pl.loop(0, pieces)
        def _(p):
            for target in range(4):
                border(p, target, True).wait_send()
        finish()


def hub_program(spectrum, cells, offsets, counts, tables):
    components, _, planes, rows_y, width = spectrum.shape
    slots = cells.shape[1]
    lines = rows_y // (2 * SUB)
    pieces = components * planes
    chunks = pieces * SUB
    factor, tcos, tsin, whi, wlo, perm = tables
    sign = np.ones((2, 8, 1), np.float32)
    sign[1, 1::2] = -1.0
    factor = factor.reshape(2, 4, width)
    tcos, tsin = tcos[None] * sign, tsin[None] * sign
    dma = pltpu.SemaphoreType.DMA
    vmem = pl.BlockSpec(memory_space=pltpu.VMEM)
    out, values = pl.pallas_call(
        hub_kernel,
        out_shape=(jax.ShapeDtypeStruct((components, planes, rows_y, width), F32),
                   jax.ShapeDtypeStruct((components, slots), F32)),
        in_specs=[pl.BlockSpec(memory_space=pl.ANY), pl.BlockSpec(memory_space=pltpu.SMEM)]
        + [vmem] * 8,
        out_specs=(pl.BlockSpec(memory_space=pl.ANY), vmem),
        scratch_shapes=[
            pltpu.VMEM((chunks, 4, 2, lines, width), F32),
            pltpu.VMEM((8 * lines, 2 * width), BF16),
            pltpu.VMEM((8 * lines, 2 * width), BF16),
            pltpu.VMEM((LAG + 1, 8 * lines, width // 2), F32),
            pltpu.VMEM((chunks, 8 * lines, width // 2), F32),
            pltpu.VMEM((chunks, 8 * lines, width // 2), F32),
            pltpu.VMEM((chunks, 2, 8 * lines), F32),
            pltpu.VMEM((chunks, 2, 8 * lines), F32),
            pltpu.VMEM((chunks, 4, lines, width + 128), F32),
            pltpu.VMEM((pieces, rows_y, width + 128), F32),
            pltpu.VMEM((pieces, 2, 8, width + 128), F32),
            pltpu.VMEM((2 * (rows_y + 16), width + 128), BF16),
            pltpu.VMEM((width + 128, slots), BF16),
            pltpu.VMEM((width + 128, slots), BF16),
            pltpu.VMEM((rows_y + 16, slots), F32),
            pltpu.VMEM((planes, 1, slots), F32),
            pltpu.VMEM((components, 1, slots), F32),
            dma((chunks, 3)),
            dma((chunks, 4)),
            dma((chunks,)),
            dma((chunks,)),
            dma((chunks,)),
            dma((chunks,)),
            dma((chunks, 3)),
            dma((chunks, 2)),
            dma((chunks,)),
            dma((chunks,)),
            dma((pieces, 4)),
            dma((pieces, 2)),
            dma((pieces,)),
        ],
        compiler_params=pltpu.CompilerParams(
            collective_id=0, has_side_effects=True, vmem_limit_bytes=63 << 20),
    )(spectrum, counts, cells, offsets, factor, tcos, tsin, whi, wlo, perm)
    return out, values


def general_transform(real, imag):
    parts, lines, width = real.shape
    length = parts * width
    k = np.arange(length, dtype=np.float64)
    symbol = (4.0 + 2.0 * np.cos(k * (2.0 * math.pi / length))) / 6.0
    factor = (1.0 / (symbol * math.sqrt(length))).reshape(parts, 1, width).astype(np.float32)
    real, imag = real * factor, imag * factor
    highest = lax.Precision.HIGHEST

    def table(left, right, modulus):
        angle = (np.outer(np.arange(left), np.arange(right)) % modulus) * (2 * math.pi / modulus)
        return np.cos(angle).astype(np.float32), np.sin(angle).astype(np.float32)

    c, s = table(parts, parts, parts)
    first = functools.partial(jnp.einsum, "ilk,im->mlk", precision=highest)
    yr, yi = first(real, c) - first(imag, s), first(real, s) + first(imag, c)
    c, s = table(parts, width, length)
    c, s = c[:, None], s[:, None]
    zr, zi = yr * c - yi * s, yr * s + yi * c
    c, s = table(width, width, width)
    last = functools.partial(jnp.einsum, "mlk,kq->lqm", precision=highest)
    out = (last(zr, c) - last(zi, s)).reshape(lines, parts, width)
    return jnp.moveaxis(out, 1, 0)


def spline_weights(frac):
    cube = frac * frac * frac
    square = frac * frac
    first = (1.0 - frac) * (1.0 - frac) * (1.0 - frac) / 6.0
    second = (3.0 * cube - 6.0 * square + 4.0) / 6.0
    third = (-3.0 * cube + 3.0 * square + 3.0 * frac + 1.0) / 6.0
    fourth = cube / 6.0
    return [first, second, third, fourth]


def dense(distance, weights):
    total = jnp.zeros(distance.shape, F32)
    for tap in range(4):
        total = jnp.where(distance == tap, weights[tap], total)
    return total


def halo_place(rows, size, chunk):
    h = lax.broadcasted_iota(jnp.int32, (rows, chunk), 0)
    return jnp.where(h < 3, h - 3, jnp.where(h < 6, h + (size - 3), -1000000))


def point_kernel(planes, count_ref, near_ref, off_ref, main_ref, zh_ref, yh_ref, cor_ref,
                 out_ref, fhi, flo, whi, wlo, wy_ref):
    block, width = main_ref.shape[0] // 3, main_ref.shape[1]
    rows_y = block // planes
    chunk = near_ref.shape[1]
    body = 3 * block

    @pl.when(pl.program_id(0) == 0)
    def _():
        for c in range(3):
            @pl.loop(0, planes)
            def _(x):
                dst = pl.ds(pl.multiple_of(c * block + x * rows_y, rows_y), rows_y)
                hi, lo = split(main_ref[dst, :])
                fhi[dst, 0:width] = hi
                flo[dst, 0:width] = lo
                hi, lo = split(zh_ref[dst, :])
                fhi[dst, width:] = hi
                flo[dst, width:] = lo
        hi, lo = split(yh_ref[...])
        fhi[body:, 0:width] = hi
        flo[body:, 0:width] = lo
        hi, lo = split(cor_ref[...])
        fhi[body:, width:] = hi
        flo[body:, width:] = lo

    wx = spline_weights(off_ref[0:1, :])
    wy = spline_weights(off_ref[1:2, :])
    wz = spline_weights(off_ref[2:3, :])
    first_y = near_ref[0:1, :] - 1
    first_z = near_ref[1:2, :] - 1
    for tile in range(width // 128):
        place = lax.broadcasted_iota(jnp.int32, (128, chunk), 0) + tile * 128
        hi, lo = split(dense(place - first_z, wz))
        whi[tile * 128 : tile * 128 + 128, :] = hi
        wlo[tile * 128 : tile * 128 + 128, :] = lo
    hi, lo = split(dense(halo_place(128, width, chunk) - first_z, wz))
    whi[width:, :] = hi
    wlo[width:, :] = lo
    place = lax.broadcasted_iota(jnp.int32, (rows_y, chunk), 0)
    wy_ref[0:rows_y, :] = dense(place - first_y, wy)
    wy_ref[rows_y:, :] = dense(halo_place(8, rows_y, chunk) - first_y, wy)

    def layer(begin, rows):
        high = fhi[begin : begin + rows, :]
        return (dot(high, whi[...]) + dot(flo[begin : begin + rows, :], whi[...])
                + dot(high, wlo[...]))

    slot = lax.broadcasted_iota(jnp.int32, (1, chunk), 1) + pl.program_id(0) * chunk
    live = slot < count_ref[0]
    edge = layer(body, 3 * planes * 8)
    for c in range(3):
        inner = layer(c * block, block)
        value = jnp.zeros((1, chunk), F32)
        for x in range(planes):
            part = jnp.sum(inner[x * rows_y : (x + 1) * rows_y] * wy_ref[0:rows_y, :], axis=0,
                           keepdims=True)
            at = (c * planes + x) * 8
            part = part + jnp.sum(edge[at : at + 8] * wy_ref[rows_y:, :], axis=0, keepdims=True)
            value = value + part * wx[x]
        out_ref[c : c + 1, :] = jnp.where(live, value, 0.0)


def sample(counts, near, offsets, main, zh, yh, cor, planes):
    slots = near.shape[1]
    block, width = main.shape[0] // 3, main.shape[1]
    rows_y = block // planes
    chunk = math.gcd(slots, 256)
    whole = pl.BlockSpec(memory_space=pltpu.VMEM)
    return pl.pallas_call(
        functools.partial(point_kernel, planes),
        out_shape=jax.ShapeDtypeStruct((3, slots), F32),
        grid=(slots // chunk,),
        in_specs=[
            pl.BlockSpec(memory_space=pltpu.SMEM),
            pl.BlockSpec((2, chunk), lambda i: (0, i)),
            pl.BlockSpec((3, chunk), lambda i: (0, i)),
        ] + [whole] * 4,
        out_specs=pl.BlockSpec((3, chunk), lambda i: (0, i)),
        scratch_shapes=[
            pltpu.VMEM((3 * block + 24 * planes, width + 128), BF16),
            pltpu.VMEM((3 * block + 24 * planes, width + 128), BF16),
            pltpu.VMEM((width + 128, chunk), BF16),
            pltpu.VMEM((width + 128, chunk), BF16),
            pltpu.VMEM((rows_y + 8, chunk), F32),
        ],
        compiler_params=pltpu.CompilerParams(vmem_limit_bytes=32 << 20),
    )(counts, near, offsets, main, zh, yh, cor)


def ring(axis):
    count = lax.axis_size(axis)
    forward = [(i, (i + 1) % count) for i in range(count)]
    return forward, [(b, a) for a, b in forward]


def per_device(spectrum, cells, offsets, counts):
    components, halves, planes, rows_y, rows_z = spectrum.shape
    parts = lax.axis_size("gz")
    length_z = rows_z * parts
    length_y = rows_y * lax.axis_size("gy")
    z_start = lax.axis_index("gz") * rows_z
    y_start = lax.axis_index("gy") * rows_y
    lines = planes * rows_y // parts
    tiled = rows_z % (parts * 64) == 0 and lines % 16 == 0
    tables = line_tables(parts, rows_z) if tiled else None
    exchange = functools.partial(
        lax.all_to_all, axis_name="gz", split_axis=0, concat_axis=0, tiled=True)
    if (parts == 8 and tiled and rows_y == 128 and planes == 4 and lax.axis_size("gy") > 2
            and cells.shape[1] % (256 * SUB) == 0 and cells.shape[1] // 256 <= 8):
        return hub_program(spectrum, cells, offsets, counts, tables)
    blocks = []
    for c in range(components):
        real = exchange(spectrum[c, 0].reshape(parts, lines, rows_z))
        imag = exchange(spectrum[c, 1].reshape(parts, lines, rows_z))
        done = transform(real, imag, tables) if tiled else general_transform(real, imag)
        blocks.append(exchange(done).reshape(planes, rows_y, rows_z))
    coefficients = jnp.stack(blocks)
    pieces = components * planes
    field = coefficients.reshape(pieces, rows_y, rows_z)

    forward, backward = ring("gz")
    flat_low = jnp.swapaxes(field[:, :, rows_z - 3 :], 1, 2)
    flat_high = jnp.swapaxes(field[:, :, :3], 1, 2)
    z_halo = jnp.concatenate(
        [lax.ppermute(flat_low, "gz", forward), lax.ppermute(flat_high, "gz", backward)], axis=1)
    forward, backward = ring("gy")
    y_low = lax.ppermute(field[:, rows_y - 3 :], "gy", forward)
    y_high = lax.ppermute(field[:, :3], "gy", backward)
    c_low = lax.ppermute(z_halo[:, :, rows_y - 3 :], "gy", forward)
    c_high = lax.ppermute(z_halo[:, :, :3], "gy", backward)
    y_halo = jnp.concatenate([y_low, y_high, jnp.zeros((pieces, 2, rows_z), F32)], axis=1)
    corner = jnp.concatenate([c_low, c_high, jnp.zeros((pieces, 6, 2), F32)], axis=2)

    def wide(item):
        item = jnp.swapaxes(item, 1, 2)
        return jnp.pad(item, ((0, 0), (0, 0), (0, 122))).reshape(-1, 128)

    near_y = (cells[0] - y_start + 2) % length_y - 2
    near_z = (cells[1] - z_start + 2) % length_z - 2
    interpolated = sample(
        counts, jnp.stack([near_y, near_z]), offsets,
        field.reshape(pieces * rows_y, rows_z),
        wide(z_halo), y_halo.reshape(pieces * 8, rows_z), wide(corner), planes)
    return (coefficients, interpolated)


def solution(mesh):
    placed = (
        P(None, None, None, "gy", "gz"),
        P(None, ("gz", "gy")),
        P(None, ("gz", "gy")),
        P(("gz", "gy")),
    )
    return jax.shard_map(
        per_device,
        mesh=mesh,
        in_specs=placed,
        out_specs=(P(None, None, "gy", "gz"), P(None, ("gz", "gy"))),
        check_vma=False,
    )
```

```python
import functools
import math

import jax
import jax.numpy as jnp
import numpy as np
from jax import lax
from jax.experimental import pallas as pl
from jax.experimental.pallas import tpu as pltpu
from jax.sharding import PartitionSpec as P

F32 = jnp.float32
BF16 = jnp.bfloat16


def split(value):
    high = value.astype(BF16)
    return high, (value - high.astype(F32)).astype(BF16)


def split_table(table):
    high = np.asarray(table, np.float32).astype(BF16)
    low = (table - high.astype(np.float64)).astype(np.float32).astype(BF16)
    return high, low


def dot(left, right):
    return jnp.dot(left, right, preferred_element_type=F32)


def dft(items):
    count = len(items)
    if count == 1:
        return items
    even = dft(items[0::2])
    odd = dft(items[1::2])
    half = count // 2
    low, high = [], []
    for m in range(half):
        er, ei = even[m]
        xr, xi = odd[m]
        if m == 0:
            tr, ti = xr, xi
        elif 4 * m == count:
            tr, ti = -xi, xr
        elif 8 * m == count:
            s = math.sqrt(0.5)
            tr, ti = (xr - xi) * s, (xr + xi) * s
        elif 8 * m == 3 * count:
            s = math.sqrt(0.5)
            tr, ti = (xr + xi) * -s, (xr - xi) * s
        else:
            c, s = math.cos(2 * math.pi * m / count), math.sin(2 * math.pi * m / count)
            tr, ti = xr * c - xi * s, xr * s + xi * c
        low.append((er + tr, ei + ti))
        high.append((er - tr, ei - ti))
    return low + high


def line_kernel(re_ref, im_ref, factor_ref, tcos_ref, tsin_ref, whi_ref, wlo_ref, perm_ref,
                out_ref, yhi_ref, ylo_ref, z_ref):
    parts, lines, width = re_ref.shape
    step = 16

    @pl.loop(0, lines // step)
    def _(group):
        rows = pl.ds(pl.multiple_of(group * step, step), step)
        for tile in range(width // 128):
            lanes = slice(tile * 128, tile * 128 + 128)
            items = []
            for i in range(parts):
                f = factor_ref[i : i + 1, lanes]
                items.append((re_ref[i, rows, lanes] * f, im_ref[i, rows, lanes] * f))
            for m, (yr, yi) in enumerate(dft(items)):
                c, s = tcos_ref[m : m + 1, lanes], tsin_ref[m : m + 1, lanes]
                zr, zi = yr * c - yi * s, yr * s + yi * c
                shifted = slice(width + tile * 128, width + tile * 128 + 128)
                hi, lo = split(zr)
                yhi_ref[m, rows, lanes] = hi
                ylo_ref[m, rows, lanes] = lo
                hi, lo = split(zi)
                yhi_ref[m, rows, shifted] = hi
                ylo_ref[m, rows, shifted] = lo

    @pl.loop(0, parts)
    def _(m):
        yhi = yhi_ref[m]
        z_ref[m] = dot(yhi, whi_ref[...]) + dot(ylo_ref[m], whi_ref[...]) + dot(yhi, wlo_ref[...])

    each = width // parts
    for target in range(parts):
        lanes = slice(target * each, target * each + each)
        joined = jnp.concatenate([z_ref[m, :, lanes] for m in range(parts)], axis=1)
        hi, lo = split(joined)
        out_ref[target] = dot(hi, perm_ref[...]) + dot(lo, perm_ref[...])


def transform(real, imag, tables):
    parts, lines, width = real.shape
    return pl.pallas_call(
        line_kernel,
        out_shape=jax.ShapeDtypeStruct((parts, lines, width), F32),
        in_specs=[pl.BlockSpec(memory_space=pltpu.VMEM)] * 8,
        out_specs=pl.BlockSpec(memory_space=pltpu.VMEM),
        scratch_shapes=[
            pltpu.VMEM((parts, lines, 2 * width), BF16),
            pltpu.VMEM((parts, lines, 2 * width), BF16),
            pltpu.VMEM((parts, lines, width), F32),
        ],
        compiler_params=pltpu.CompilerParams(vmem_limit_bytes=24 << 20),
        cost_estimate=pl.CostEstimate(
            flops=20 * parts * lines * width * width, bytes_accessed=12 * parts * lines * width,
            transcendentals=0),
    )(real, imag, *tables)


def line_tables(parts, width):
    length = parts * width
    k = np.arange(length, dtype=np.float64)
    symbol = (4.0 + 2.0 * np.cos(k * (2.0 * math.pi / length))) / 6.0
    factor = (1.0 / (symbol * math.sqrt(length))).reshape(parts, width).astype(np.float32)
    turn = np.outer(np.arange(parts), np.arange(width)) * (2.0 * math.pi / length)
    angle = (np.outer(np.arange(width), np.arange(width)) % width) * (2.0 * math.pi / width)
    whi, wlo = split_table(np.concatenate([np.cos(angle), -np.sin(angle)], axis=0))
    each = width // parts
    perm = np.zeros((width, width), np.float32)
    for m in range(parts):
        for q in range(each):
            perm[m * each + q, parts * q + m] = 1.0
    made = (factor, np.cos(turn).astype(np.float32), np.sin(turn).astype(np.float32),
            whi, wlo, perm.astype(BF16))
    return made


MESH = pl.DeviceIdType.MESH


SUB = 4
DIRECT = 2
AHEAD = 2
EARLY = 6
LAG = 2
DEPTH = 2


def hub_kernel(spec, count_ref, cells, offs, *rest):
    sources, (out, vals), tables, held = rest[:6], rest[6:8], rest[8:14], rest[14:]
    hub_body(spec, count_ref, cells, offs, sources, tables, out, vals, *held)


def hub_body(spec, count_ref, cells, offs, sources, tables, out, vals, table_s,
               xbuf, yhi, ylo, zown, zsend, zrecv, rim_out, rim_in, total, field, halo_y,
               fboth, pzhi, pzlo, py, wxs, acc,
               send_a, recv_a, cross_s, cross_r, rim_s, rim_r, dist_s, dist_r, loc, keep,
               halo_s, halo_r, out_s):
    factor, tcos, tsin, whi, wlo, perm = tables
    components, _, planes, rows_y, width = spec.shape
    lines = rows_y // (2 * SUB)
    pieces = components * planes
    chunks = pieces * SUB
    slots = cells.shape[1]
    chunk = 256
    groups = slots // chunk
    share = groups // SUB
    parts = 8
    each = width // parts
    wide = width // 2
    body = rows_y + 16
    me = lax.axis_index("gz")
    half = me // 4
    side = me % 2
    is_hub = ((me // 2) == 1) | ((me // 2) == 2)
    hub_same = 2 + 2 * half + side
    hub_other = 2 + 2 * half + (1 - side)
    leaf_same = 6 * half + side
    leaf_other = 6 * half + (1 - side)
    partner = 4 - 2 * half + side
    gy, gy_count = lax.axis_index("gy"), lax.axis_size("gy")
    y_next, y_prev = lax.rem(gy + 1, gy_count), lax.rem(gy + gy_count - 1, gy_count)

    barrier = pltpu.get_barrier_semaphore()

    def greet(peer):
        pl.semaphore_signal(barrier, inc=1, device_id=peer, device_id_type=MESH)

    greet({"gz": 2 + 2 * half, "gy": y_next})
    greet({"gz": 3 + 2 * half, "gy": y_prev})

    @pl.when(is_hub)
    def _():
        for peer in (leaf_same, leaf_other, hub_other, partner):
            greet({"gz": peer})
        beside = jnp.where(side == 1, y_next, y_prev)
        for target in range(4):
            greet({"gz": 4 * half + target, "gy": beside})

    @pl.when(jnp.logical_not(is_hub))
    def _():
        for peer in (hub_same, hub_other, leaf_other):
            greet({"gz": peer})

    def rows_of(j, which):
        return pl.ds(pl.multiple_of(which * (lines * SUB) + (j % SUB) * lines, lines), lines)

    def remote(source, target, send, recv, peer):
        return pltpu.make_async_remote_copy(
            src_ref=source, dst_ref=target, send_sem=send, recv_sem=recv,
            device_id=peer if isinstance(peer, dict) else {"gz": peer}, device_id_type=MESH)

    def source(j, which):
        piece = j // SUB
        return spec.at[piece // planes, :, piece % planes, rows_of(j, which), :]

    def give(j, which, n, peer):
        return remote(source(j, which),
                      xbuf.at[j, me % 4], send_a.at[j, n], recv_a.at[j, me % 4], peer)

    def relay(j):
        slot = leaf_other % 4
        return remote(xbuf.at[j, slot], xbuf.at[j, slot], send_a.at[j, 2], recv_a.at[j, slot],
                      hub_same)

    def arrival(j, slot):
        return remote(xbuf.at[j, slot], xbuf.at[j, slot], send_a.at[j, 0], recv_a.at[j, slot],
                      partner)

    def own(j):
        return pltpu.make_async_copy(source(j, side),
                                     xbuf.at[j, me % 4], loc.at[j])

    def cross(j):
        return remote(zsend.at[j], zrecv.at[j], cross_s.at[j], cross_r.at[j], partner)

    def rim(j):
        return remote(rim_out.at[j], rim_in.at[j], rim_s.at[j], rim_r.at[j], partner)

    def place(j, which):
        return field.at[j // SUB, rows_of(j, which), :]

    def hand(j, n, peer):
        return remote(total.at[j, peer % 4], place(j, side), dist_s.at[j, n],
                      dist_r.at[j, side], peer)

    def taken(j, which):
        return remote(total.at[j, 0], place(j, which), dist_s.at[j, 0], dist_r.at[j, which],
                      hub_other)

    def kept(j):
        return pltpu.make_async_copy(total.at[j, me % 4], place(j, side), keep.at[j])

    def border(p, target, last):
        if last:
            rows, peer = total.at[p * SUB + SUB - 1, target, lines - 8 :, :], y_next
        else:
            rows, peer = total.at[p * SUB, target, 0:8, :], y_prev
        at = 0 if last else 1
        return remote(rows, halo_y.at[p, at], halo_s.at[p, target], halo_r.at[p, at],
                      {"gz": 4 * half + target, "gy": peer})

    def out_copy(p):
        return pltpu.make_async_copy(field.at[p, :, 0:width], out.at[p // planes, p % planes],
                                     out_s.at[p])

    def prepare(p):
        @pl.when(is_hub)
        def _():
            @pl.loop(0, SUB)
            def _(n):
                kept(p * SUB + n).wait()

        @pl.when(jnp.logical_not(is_hub))
        def _():
            @pl.loop(0, SUB)
            def _(n):
                taken(p * SUB + n, side).wait_recv()

        @pl.loop(0, SUB)
        def _(n):
            taken(p * SUB + n, 1 - side).wait_recv()
        out_copy(p).start()
        border(p, 0, True).wait_recv()
        border(p, 0, False).wait_recv()
        fboth[0:rows_y], fboth[body : body + rows_y] = split(field[p])
        fboth[rows_y:body], fboth[body + rows_y :] = split(
            jnp.concatenate([halo_y[p, 0], halo_y[p, 1]], axis=0))

    def lanes_of(u):
        return pl.ds(pl.multiple_of(u * chunk, chunk), chunk)

    def first_cell(row, start, length, at):
        near = cells[row : row + 1, at] - (start - 2)
        near = jnp.where(near < 0, near + length, near)
        return jnp.where(near >= length, near - length, near) - 3

    def weigh(u):
        at = lanes_of(u)
        for x, weight in enumerate(spline_weights(offs[0:1, at])):
            wxs[x, :, at] = weight
        wy = spline_weights(offs[1:2, at])
        wz = spline_weights(offs[2:3, at])
        first_y = first_cell(0, gy * rows_y, gy_count * rows_y, at)
        first_z = first_cell(1, me * width, 8 * width, at)

        @pl.loop(0, width // 32)
        def _(tile):
            spot = lax.broadcasted_iota(jnp.int32, (32, chunk), 0) + tile * 32
            rows = pl.ds(pl.multiple_of(tile * 32, 32), 32)
            pzhi[rows, at], pzlo[rows, at] = split(dense(spot - first_z, wz))
        h = lax.broadcasted_iota(jnp.int32, (16, chunk), 0)
        spot = jnp.where(h < 8, h - 8, h + (width - 8))
        pzhi[width : width + 16, at], pzlo[width : width + 16, at] = split(
            dense(spot - first_z, wz))
        zero = jnp.zeros((112, chunk), BF16)
        pzhi[width + 16 :, at] = zero
        pzlo[width + 16 :, at] = zero

        @pl.loop(0, (rows_y + 16) // 16)
        def _(tile):
            spot = lax.broadcasted_iota(jnp.int32, (16, chunk), 0) + (tile * 16 - 8)
            rows = pl.ds(pl.multiple_of(tile * 16, 16), 16)
            py[rows, at] = dense(spot - first_y, wy)

    def interpolate(p, u):
        c, x = p // planes, p % planes
        at = lanes_of(u)
        both = dot(fboth[...], pzhi[:, at])
        field_z = both[0:body] + both[body:] + dot(fboth[0:body], pzlo[:, at])
        value = jnp.sum(field_z[0:rows_y] * py[8 : 8 + rows_y, at], axis=0, keepdims=True)
        ends = (field_z[rows_y : rows_y + 8] * py[0:8, at]
                + field_z[rows_y + 8 :] * py[8 + rows_y :, at])
        value = (value + jnp.sum(ends, axis=0, keepdims=True)) * wxs[x, :, at]
        acc[c, :, at] = acc[c, :, at] + value

    def finish():
        slot = lax.broadcasted_iota(jnp.int32, (1, slots), 1)
        for c in range(components):
            vals[c : c + 1, :] = jnp.where(slot < count_ref[0], acc[c], 0.0)

        @pl.loop(0, pieces)
        def _(p):
            out_copy(p).wait()

    def spread(step):
        p, turn = step // SUB, step % SUB

        @pl.when(turn == 0)
        def _():
            prepare(p)

        @pl.loop(0, share)
        def _(n):
            interpolate(p, turn * share + n)

    acc[...] = jnp.zeros(acc.shape, F32)
    table_copies = [pltpu.make_async_copy(source, table, table_s.at[n])
                    for n, (source, table) in enumerate(zip(sources, tables))]

    @pl.when(is_hub)
    def _():
        @pl.loop(0, chunks)
        def _(j):
            own(j).start()
        for copy in table_copies:
            copy.start()

    @pl.when(jnp.logical_not(is_hub))
    def _():
        pl.semaphore_wait(barrier, 5)

        @pl.loop(DIRECT, EARLY)
        def _(j):
            give(j, 1 - side, 1, leaf_other).start()

        first_step = SUB + LAG + DEPTH + 4

        def same(j):
            return give(j, side, 0, hub_same)

        def sent(j):
            same(j).wait_send()
            give(j, 1 - side, 1, hub_other).wait_send()

            @pl.when(j >= DIRECT)
            def _():
                relay(j).wait_send()

        def pass_on(j):
            @pl.when(j >= DEPTH)
            def _():
                sent(j - DEPTH)

            same(j).start()

            @pl.when(j + EARLY < chunks)
            def _():
                give(j + EARLY, 1 - side, 1, leaf_other).start()

            @pl.when(j < DIRECT)
            def _():
                give(j, 1 - side, 1, hub_other).start()

            @pl.when(j >= DIRECT)
            def _():
                arrival(j, leaf_other % 4).wait_recv()
                relay(j).start()

        @pl.loop(0, chunks + first_step)
        def _(t):
            @pl.when(t < chunks)
            def _():
                pass_on(t)

            @pl.when(t < groups)
            def _():
                weigh(t)

            @pl.when(t >= first_step)
            def _():
                spread(t - first_step)

        @pl.loop(chunks - DEPTH, chunks)
        def _(j):
            sent(j)
        finish()

    def first_stage(j):
        own(j).wait()
        arrival(j, leaf_same % 4).wait_recv()
        arrival(j, leaf_other % 4).wait_recv()
        arrival(j, hub_other % 4).wait_recv()
        root = math.sqrt(0.5)

        @pl.loop(0, lines // 16)
        def _(group):
            rows = pl.ds(pl.multiple_of(group * 16, 16), 16)
            for tile in range(width // 128):
                lanes = slice(tile * 128, tile * 128 + 128)
                items = []
                for i in range(4):
                    f = factor[half, i : i + 1, lanes]
                    items.append((xbuf[j, i, 0, rows, lanes] * f, xbuf[j, i, 1, rows, lanes] * f))
                (ar, ai), (br, bi), (cr, ci), (dr, di) = items
                turned = [(ar, ai), ((br - bi) * root, (br + bi) * root), (-ci, cr),
                          ((dr + di) * -root, (dr - di) * root)]
                even, odd = dft(items), dft(turned)
                for m in range(parts):
                    yr, yi = (odd if m % 2 else even)[m // 2]
                    c, s = tcos[half, m : m + 1, lanes], tsin[half, m : m + 1, lanes]
                    zr, zi = yr * c - yi * s, yr * s + yi * c
                    at = pl.ds(pl.multiple_of(m * lines + group * 16, 16), 16)
                    shifted = slice(width + tile * 128, width + tile * 128 + 128)
                    hi, lo = split(zr)
                    yhi[at, lanes] = hi
                    ylo[at, lanes] = lo
                    hi, lo = split(zi)
                    yhi[at, shifted] = hi
                    ylo[at, shifted] = lo

        def product(which):
            lanes = pl.ds(pl.multiple_of(which * wide, wide), wide)
            left = yhi[...]
            return dot(left, whi[:, lanes]) + dot(ylo[...], whi[:, lanes]) + dot(left, wlo[:, lanes])

        zsend[j] = product(1 - half)
        cross(j).start()
        kept_part = product(half)
        zown[j % (LAG + 1)] = kept_part
        rim_out[j] = jnp.concatenate([jnp.transpose(kept_part[:, wide - 128 :])[127:128],
                                      jnp.transpose(kept_part[:, 0:128])[0:1]], axis=0)
        rim(j).start()

    def second_stage(j):
        cross(j).wait_recv()
        rim(j).wait_recv()
        mine = j % (LAG + 1)
        targets = []
        for target in range(4):
            lanes = slice(target * each, target * each + each)
            terms = []
            for m in range(parts):
                rows = slice(m * lines, m * lines + lines)
                terms.append(zown[mine, rows, lanes] + zrecv[j, rows, lanes])
            targets.append(jnp.concatenate(terms, axis=1))
        count = parts * lines
        lane = lax.broadcasted_iota(jnp.int32, (count, 128), 1)
        theirs = jnp.transpose(jnp.concatenate([rim_in[j], jnp.zeros((126, count), F32)], axis=0))
        ends = theirs + jnp.where(
            lane == 0, pltpu.roll(zsend[j, :, wide - 128 :], 1, 1),
            jnp.where(lane == 1, pltpu.roll(zsend[j, :, 0:128], 1, 1), 0.0))
        targets.append(jnp.concatenate(
            [ends[m * lines : m * lines + lines, 0:each] for m in range(parts)], axis=1))
        hi, lo = split(jnp.concatenate(targets, axis=0))
        both = dot(jnp.concatenate([hi, lo], axis=0), perm[...])
        full = both[0 : 5 * lines] + both[5 * lines :]
        ends = full[4 * lines :, 0:128]
        lane = lax.broadcasted_iota(jnp.int32, (lines, 128), 1)
        for target in range(4):
            at = target * lines
            low = ends if target == 0 else pltpu.roll(full[at - lines : at, width - 128 :], 8, 1)
            high = ends if target == 3 else pltpu.roll(full[at + lines : at + 2 * lines, 0:128], 8, 1)
            total[j, target, :, 0:width] = full[at : at + lines]
            total[j, target, :, width:] = jnp.where(
                lane < 8, low, jnp.where(lane < 16, high, 0.0))
        hand(j, 0, leaf_same).start()
        hand(j, 1, leaf_other).start()
        hand(j, 2, hub_other).start()
        kept(j).start()

        @pl.when((side == 1) & (j % SUB == SUB - 1))
        def _():
            for target in range(4):
                border(j // SUB, target, True).start()

        @pl.when((side == 0) & (j % SUB == 0))
        def _():
            for target in range(4):
                border(j // SUB, target, False).start()

    @pl.when(is_hub)
    def _():
        pl.semaphore_wait(barrier, 10)

        @pl.loop(0, AHEAD)
        def _(j):
            give(j, 1 - side, 0, hub_other).start()

        for copy in table_copies:
            copy.wait()
        first_step = SUB + LAG + 2
        steps = chunks + LAG

        @pl.loop(0, steps)
        def _(t):
            @pl.when(t < chunks)
            def _():
                first_stage(t)

            @pl.when(t + AHEAD < chunks)
            def _():
                give(t + AHEAD, 1 - side, 0, hub_other).start()

            @pl.when(t >= LAG)
            def _():
                second_stage(t - LAG)

            @pl.when(t < groups)
            def _():
                weigh(t)

            @pl.when(t >= first_step)
            def _():
                spread(t - first_step)

        @pl.loop(steps - first_step, chunks)
        def _(step):
            spread(step)

        @pl.loop(0, chunks)
        def _(j):
            give(j, 1 - side, 0, hub_other).wait_send()
            cross(j).wait_send()
            rim(j).wait_send()
            hand(j, 0, leaf_same).wait_send()
            hand(j, 1, leaf_other).wait_send()
            hand(j, 2, hub_other).wait_send()

        @pl.loop(0, pieces)
        def _(p):
            for target in range(4):
                border(p, target, True).wait_send()
        finish()


def hub_program(spectrum, cells, offsets, counts, tables):
    components, _, planes, rows_y, width = spectrum.shape
    slots = cells.shape[1]
    lines = rows_y // (2 * SUB)
    pieces = components * planes
    chunks = pieces * SUB
    factor, tcos, tsin, whi, wlo, perm = tables
    sign = np.ones((2, 8, 1), np.float32)
    sign[1, 1::2] = -1.0
    factor = factor.reshape(2, 4, width)
    tcos, tsin = tcos[None] * sign, tsin[None] * sign
    dma = pltpu.SemaphoreType.DMA
    vmem = pl.BlockSpec(memory_space=pltpu.VMEM)
    hbm = pl.BlockSpec(memory_space=pltpu.HBM)
    out, values = pl.pallas_call(
        hub_kernel,
        out_shape=(pltpu.VMEM((components, planes, rows_y, width), F32),
                   pltpu.VMEM((components, slots), F32)),
        in_specs=[hbm, pl.BlockSpec(memory_space=pltpu.SMEM), vmem, vmem] + [hbm] * 6,
        out_specs=(vmem, vmem),
        scratch_shapes=[
            pltpu.VMEM((2, 4, width), F32),
            pltpu.VMEM((2, 8, width), F32),
            pltpu.VMEM((2, 8, width), F32),
            pltpu.VMEM((2 * width, width), BF16),
            pltpu.VMEM((2 * width, width), BF16),
            pltpu.VMEM((width, width), BF16),
            dma((6,)),
            pltpu.VMEM((chunks, 4, 2, lines, width), F32),
            pltpu.VMEM((8 * lines, 2 * width), BF16),
            pltpu.VMEM((8 * lines, 2 * width), BF16),
            pltpu.VMEM((LAG + 1, 8 * lines, width // 2), F32),
            pltpu.VMEM((chunks, 8 * lines, width // 2), F32),
            pltpu.VMEM((chunks, 8 * lines, width // 2), F32),
            pltpu.VMEM((chunks, 2, 8 * lines), F32),
            pltpu.VMEM((chunks, 2, 8 * lines), F32),
            pltpu.VMEM((chunks, 4, lines, width + 128), F32),
            pltpu.VMEM((pieces, rows_y, width + 128), F32),
            pltpu.VMEM((pieces, 2, 8, width + 128), F32),
            pltpu.VMEM((2 * (rows_y + 16), width + 128), BF16),
            pltpu.VMEM((width + 128, slots), BF16),
            pltpu.VMEM((width + 128, slots), BF16),
            pltpu.VMEM((rows_y + 16, slots), F32),
            pltpu.VMEM((planes, 1, slots), F32),
            pltpu.VMEM((components, 1, slots), F32),
            dma((chunks, 3)),
            dma((chunks, 4)),
            dma((chunks,)),
            dma((chunks,)),
            dma((chunks,)),
            dma((chunks,)),
            dma((chunks, 3)),
            dma((chunks, 2)),
            dma((chunks,)),
            dma((chunks,)),
            dma((pieces, 4)),
            dma((pieces, 2)),
            dma((pieces,)),
        ],
        compiler_params=pltpu.CompilerParams(
            collective_id=0, has_side_effects=True, vmem_limit_bytes=56 << 20),
    )(spectrum, counts, cells, offsets, factor, tcos, tsin, whi, wlo, perm)
    return out, values


def general_transform(real, imag):
    parts, lines, width = real.shape
    length = parts * width
    k = np.arange(length, dtype=np.float64)
    symbol = (4.0 + 2.0 * np.cos(k * (2.0 * math.pi / length))) / 6.0
    factor = (1.0 / (symbol * math.sqrt(length))).reshape(parts, 1, width).astype(np.float32)
    real, imag = real * factor, imag * factor
    highest = lax.Precision.HIGHEST

    def table(left, right, modulus):
        angle = (np.outer(np.arange(left), np.arange(right)) % modulus) * (2 * math.pi / modulus)
        return np.cos(angle).astype(np.float32), np.sin(angle).astype(np.float32)

    c, s = table(parts, parts, parts)
    first = functools.partial(jnp.einsum, "ilk,im->mlk", precision=highest)
    yr, yi = first(real, c) - first(imag, s), first(real, s) + first(imag, c)
    c, s = table(parts, width, length)
    c, s = c[:, None], s[:, None]
    zr, zi = yr * c - yi * s, yr * s + yi * c
    c, s = table(width, width, width)
    last = functools.partial(jnp.einsum, "mlk,kq->lqm", precision=highest)
    out = (last(zr, c) - last(zi, s)).reshape(lines, parts, width)
    return jnp.moveaxis(out, 1, 0)


def spline_weights(frac):
    cube = frac * frac * frac
    square = frac * frac
    first = (1.0 - frac) * (1.0 - frac) * (1.0 - frac) / 6.0
    second = (3.0 * cube - 6.0 * square + 4.0) / 6.0
    third = (-3.0 * cube + 3.0 * square + 3.0 * frac + 1.0) / 6.0
    fourth = cube / 6.0
    return [first, second, third, fourth]


def dense(distance, weights):
    total = jnp.zeros(distance.shape, F32)
    for tap in range(4):
        total = jnp.where(distance == tap, weights[tap], total)
    return total


def halo_place(rows, size, chunk):
    h = lax.broadcasted_iota(jnp.int32, (rows, chunk), 0)
    return jnp.where(h < 3, h - 3, jnp.where(h < 6, h + (size - 3), -1000000))


def point_kernel(planes, count_ref, near_ref, off_ref, main_ref, zh_ref, yh_ref, cor_ref,
                 out_ref, fhi, flo, whi, wlo, wy_ref):
    block, width = main_ref.shape[0] // 3, main_ref.shape[1]
    rows_y = block // planes
    chunk = near_ref.shape[1]
    body = 3 * block

    @pl.when(pl.program_id(0) == 0)
    def _():
        for c in range(3):
            @pl.loop(0, planes)
            def _(x):
                dst = pl.ds(pl.multiple_of(c * block + x * rows_y, rows_y), rows_y)
                hi, lo = split(main_ref[dst, :])
                fhi[dst, 0:width] = hi
                flo[dst, 0:width] = lo
                hi, lo = split(zh_ref[dst, :])
                fhi[dst, width:] = hi
                flo[dst, width:] = lo
        hi, lo = split(yh_ref[...])
        fhi[body:, 0:width] = hi
        flo[body:, 0:width] = lo
        hi, lo = split(cor_ref[...])
        fhi[body:, width:] = hi
        flo[body:, width:] = lo

    wx = spline_weights(off_ref[0:1, :])
    wy = spline_weights(off_ref[1:2, :])
    wz = spline_weights(off_ref[2:3, :])
    first_y = near_ref[0:1, :] - 1
    first_z = near_ref[1:2, :] - 1
    for tile in range(width // 128):
        place = lax.broadcasted_iota(jnp.int32, (128, chunk), 0) + tile * 128
        hi, lo = split(dense(place - first_z, wz))
        whi[tile * 128 : tile * 128 + 128, :] = hi
        wlo[tile * 128 : tile * 128 + 128, :] = lo
    hi, lo = split(dense(halo_place(128, width, chunk) - first_z, wz))
    whi[width:, :] = hi
    wlo[width:, :] = lo
    place = lax.broadcasted_iota(jnp.int32, (rows_y, chunk), 0)
    wy_ref[0:rows_y, :] = dense(place - first_y, wy)
    wy_ref[rows_y:, :] = dense(halo_place(8, rows_y, chunk) - first_y, wy)

    def layer(begin, rows):
        high = fhi[begin : begin + rows, :]
        return (dot(high, whi[...]) + dot(flo[begin : begin + rows, :], whi[...])
                + dot(high, wlo[...]))

    slot = lax.broadcasted_iota(jnp.int32, (1, chunk), 1) + pl.program_id(0) * chunk
    live = slot < count_ref[0]
    edge = layer(body, 3 * planes * 8)
    for c in range(3):
        inner = layer(c * block, block)
        value = jnp.zeros((1, chunk), F32)
        for x in range(planes):
            part = jnp.sum(inner[x * rows_y : (x + 1) * rows_y] * wy_ref[0:rows_y, :], axis=0,
                           keepdims=True)
            at = (c * planes + x) * 8
            part = part + jnp.sum(edge[at : at + 8] * wy_ref[rows_y:, :], axis=0, keepdims=True)
            value = value + part * wx[x]
        out_ref[c : c + 1, :] = jnp.where(live, value, 0.0)


def sample(counts, near, offsets, main, zh, yh, cor, planes):
    slots = near.shape[1]
    block, width = main.shape[0] // 3, main.shape[1]
    rows_y = block // planes
    chunk = math.gcd(slots, 256)
    whole = pl.BlockSpec(memory_space=pltpu.VMEM)
    return pl.pallas_call(
        functools.partial(point_kernel, planes),
        out_shape=jax.ShapeDtypeStruct((3, slots), F32),
        grid=(slots // chunk,),
        in_specs=[
            pl.BlockSpec(memory_space=pltpu.SMEM),
            pl.BlockSpec((2, chunk), lambda i: (0, i)),
            pl.BlockSpec((3, chunk), lambda i: (0, i)),
        ] + [whole] * 4,
        out_specs=pl.BlockSpec((3, chunk), lambda i: (0, i)),
        scratch_shapes=[
            pltpu.VMEM((3 * block + 24 * planes, width + 128), BF16),
            pltpu.VMEM((3 * block + 24 * planes, width + 128), BF16),
            pltpu.VMEM((width + 128, chunk), BF16),
            pltpu.VMEM((width + 128, chunk), BF16),
            pltpu.VMEM((rows_y + 8, chunk), F32),
        ],
        compiler_params=pltpu.CompilerParams(vmem_limit_bytes=32 << 20),
    )(counts, near, offsets, main, zh, yh, cor)


def ring(axis):
    count = lax.axis_size(axis)
    forward = [(i, (i + 1) % count) for i in range(count)]
    return forward, [(b, a) for a, b in forward]


def per_device(spectrum, cells, offsets, counts):
    components, halves, planes, rows_y, rows_z = spectrum.shape
    parts = lax.axis_size("gz")
    length_z = rows_z * parts
    length_y = rows_y * lax.axis_size("gy")
    z_start = lax.axis_index("gz") * rows_z
    y_start = lax.axis_index("gy") * rows_y
    lines = planes * rows_y // parts
    tiled = rows_z % (parts * 64) == 0 and lines % 16 == 0
    tables = line_tables(parts, rows_z) if tiled else None
    exchange = functools.partial(
        lax.all_to_all, axis_name="gz", split_axis=0, concat_axis=0, tiled=True)
    if (parts == 8 and tiled and rows_y == 128 and planes == 4 and lax.axis_size("gy") > 2
            and cells.shape[1] % (256 * SUB) == 0 and cells.shape[1] // 256 <= 8):
        return hub_program(spectrum, cells, offsets, counts, tables)
    blocks = []
    for c in range(components):
        real = exchange(spectrum[c, 0].reshape(parts, lines, rows_z))
        imag = exchange(spectrum[c, 1].reshape(parts, lines, rows_z))
        done = transform(real, imag, tables) if tiled else general_transform(real, imag)
        blocks.append(exchange(done).reshape(planes, rows_y, rows_z))
    coefficients = jnp.stack(blocks)
    pieces = components * planes
    field = coefficients.reshape(pieces, rows_y, rows_z)

    forward, backward = ring("gz")
    flat_low = jnp.swapaxes(field[:, :, rows_z - 3 :], 1, 2)
    flat_high = jnp.swapaxes(field[:, :, :3], 1, 2)
    z_halo = jnp.concatenate(
        [lax.ppermute(flat_low, "gz", forward), lax.ppermute(flat_high, "gz", backward)], axis=1)
    forward, backward = ring("gy")
    y_low = lax.ppermute(field[:, rows_y - 3 :], "gy", forward)
    y_high = lax.ppermute(field[:, :3], "gy", backward)
    c_low = lax.ppermute(z_halo[:, :, rows_y - 3 :], "gy", forward)
    c_high = lax.ppermute(z_halo[:, :, :3], "gy", backward)
    y_halo = jnp.concatenate([y_low, y_high, jnp.zeros((pieces, 2, rows_z), F32)], axis=1)
    corner = jnp.concatenate([c_low, c_high, jnp.zeros((pieces, 6, 2), F32)], axis=2)

    def wide(item):
        item = jnp.swapaxes(item, 1, 2)
        return jnp.pad(item, ((0, 0), (0, 0), (0, 122))).reshape(-1, 128)

    near_y = (cells[0] - y_start + 2) % length_y - 2
    near_z = (cells[1] - z_start + 2) % length_z - 2
    interpolated = sample(
        counts, jnp.stack([near_y, near_z]), offsets,
        field.reshape(pieces * rows_y, rows_z),
        wide(z_halo), y_halo.reshape(pieces * 8, rows_z), wide(corner), planes)
    return (coefficients, interpolated)


def solution(mesh):
    placed = (
        P(None, None, None, "gy", "gz"),
        P(None, ("gz", "gy")),
        P(None, ("gz", "gy")),
        P(("gz", "gy")),
    )
    return jax.shard_map(
        per_device,
        mesh=mesh,
        in_specs=placed,
        out_specs=(P(None, None, "gy", "gz"), P(None, ("gz", "gy"))),
        check_vma=False,
    )
```
